1024 devices in a mesh: grp: 4 (over y_hi), blk: 32 (over x, y_lo, core), dep: 8 (over z).
Axes of the slice: x: 8, y: 8 (y_hi: 4, y_lo: 2; y = y_hi * 2 + y_lo), z: 8, core: 2. Of those that a mesh axis runs over, the one named last changes fastest.
Arguments:
- velocity: float32 [3, 1024, 64, 128], P(None, 'blk', 'dep', 'grp'), may hold values from -6 to 6
- scalar: float32 [64, 128, 8192], P('dep', 'grp', 'blk'), may hold values from -6 to 6
- spline_base: int32 [8192], P('blk'), may hold values from -1 to 1023, as said below
- spline_frac: float32 [8192], P('blk'), may hold values from 0 to 1
Outputs:
- segment_velocity: float32 [3, 1024, 64, 128], P(None, 'blk', 'dep', 'grp')
- scalar_segment: float32 [64, 128, 8192], P('dep', 'grp', 'blk')
The draws below stay inside these ranges and needn't reach their ends.
Inputs may be any that keep to these rules, and one draw needn't show every extreme that they name: spline_base[i] is i // 8 or i // 8 - 1; the spline reads velocity cells spline_base[i] - 1 to spline_base[i] + 2 modulo 1024.
All inputs are finite; a program needn't handle non-finite values.
Results may differ from the reference program's by a relative error of at most 0.00007.
Values sent between devices are 32-bit elements; how exact they have to be, the bound alone decides.
A program may use at most 64 MiB of HBM per device.

```python
import math
import jax
import jax.numpy as jnp
from jax import lax

NX = 1024
REFINE = 8
FX = 8192
Z = 64
Y = 128


def draw_spline_base(key, part):
    cells = lax.iota(jnp.int32, FX)
    jitter = jax.random.randint(jax.random.fold_in(key, 11), (FX,), 0, 2)
    base = cells // REFINE - jitter
    base = jnp.where(cells == 0, -1, base)
    base = jnp.where(cells == FX - 1, NX - 1, base)
    return base.astype(jnp.int32)


def level_of(stream_key, dims, cuts, least, top_value):
    gain, own = 1.0, jax.random.fold_in(stream_key, 6)
    for axis_at, parts in cuts:
        heights = jnp.exp(jax.random.uniform(jax.random.fold_in(own, axis_at), (parts,), jnp.float32, least / len(cuts), top_value / len(cuts)))
        gain = gain * jnp.repeat(heights, dims[axis_at] // parts).reshape([-1 if axis == axis_at else 1 for axis in range(len(dims))])
    return gain


def scatter_about(rng, shape, scale, most, split=(), kind=jnp.bfloat16):
    result = scale * jax.random.normal(rng, shape, jnp.float32)
    if split:
        result = result * level_of(rng, shape, split, -0.22, 0.18)
    return jnp.clip(result, -most, most).astype(kind)


def setup_inputs(seed: int = 0) -> dict:
    keys = jax.random.split(jax.random.key(seed), 5)
    return {
        "velocity": scatter_about(keys[0], (3, NX, Z, Y), 1.0, 6.0, ((1, 32), (2, 8), (3, 4)), jnp.float32),
        "scalar": scatter_about(keys[1], (Z, Y, FX), 1.0, 6.0, ((0, 8), (1, 4), (2, 32)), jnp.float32),
        "spline_base": draw_spline_base(jax.random.fold_in(keys[4], 71), 0),
        "spline_frac": jnp.clip(1.0 * jax.random.uniform(keys[3], (FX,), jnp.float32) ** level_of(keys[3], (FX,), ((0, 32),), -0.2, 0.2), 0.0, 1.0),
    }


velocity_step = 0.002
viscosity = 0.00125
advect_rate = 0.2
diffuse_rate = 0.05
first_coeffs = (1.0 / 280.0, -4.0 / 105.0, 0.2, -0.8, 0.0, 0.8, -0.2, 4.0 / 105.0, -1.0 / 280.0)
second_coeffs = (-1.0 / 560.0, 8.0 / 315.0, -0.2, 1.6, -205.0 / 72.0, 1.6, -0.2, 8.0 / 315.0, -1.0 / 560.0)
highest = lax.Precision.HIGHEST


def derivative_rows(first_row, count, length):
    rows = first_row + lax.iota(jnp.int32, count)
    columns = lax.iota(jnp.int32, length)
    offset = (rows[:, None] - columns[None, :]) % length
    signed = jnp.where(offset > length // 2, offset - length, offset)
    angle = signed.astype(jnp.float32) * (math.pi / length)
    parity = 1.0 - 2.0 * (offset % 2).astype(jnp.float32)
    same = offset == 0
    sine = jnp.where(same, 1.0, jnp.sin(angle))
    first = jnp.where(same, 0.0, 0.5 * parity * jnp.cos(angle) / sine)
    second = jnp.where(same, -(length * length) / 12.0 - 1.0 / 6.0, -0.5 * parity / (sine * sine))
    average = jnp.full((count, length), 1.0 / length, jnp.float32)
    return jnp.concatenate([first, second, average], axis=0)


def catmull_weights(fraction):
    square = fraction * fraction
    cube = square * fraction
    return ((-cube + 2.0 * square - fraction) * 0.5,
            (3.0 * cube - 5.0 * square + 2.0) * 0.5,
            (-3.0 * cube + 4.0 * square + fraction) * 0.5,
            (cube - square) * 0.5)


def scalar_update(padded, fine):
    extent = (padded.shape[0] - 8, padded.shape[1] - 8, padded.shape[2] - 8)
    centre = lax.slice(padded, (4, 4, 4), (4 + extent[0], 4 + extent[1], 4 + extent[2]))
    gradients = []
    curvature = jnp.zeros(extent, jnp.float32)
    for axis_index in range(3):
        slope = jnp.zeros(extent, jnp.float32)
        for offset in range(9):
            begin = [4, 4, 4]
            begin[axis_index] = offset
            finish = (begin[0] + extent[0], begin[1] + extent[1], begin[2] + extent[2])
            window = lax.slice(padded, tuple(begin), finish)
            if first_coeffs[offset] != 0.0:
                slope = slope + first_coeffs[offset] * window
            curvature = curvature + second_coeffs[offset] * window
        gradients.append(slope)
    advection = fine[2] * gradients[0] + fine[1] * gradients[1] + fine[0] * gradients[2]
    return centre - advect_rate * advection + diffuse_rate * curvature


def reference(velocity, scalar, spline_base, spline_frac):
    length = velocity.shape[1]
    table = derivative_rows(0, length, length)
    both = jnp.einsum("kx,cxzy->ckzy", table, velocity, precision=highest)
    segment = velocity - both[:, 2 * length:] + velocity_step * (viscosity * both[:, length:2 * length] - velocity[0:1] * both[:, :length])
    weights = catmull_weights(spline_frac)
    padded = jnp.pad(scalar, 4, mode="wrap")
    depth = scalar.shape[0]

    def one_layer(layer):
        coarse = lax.dynamic_index_in_dim(segment, layer, 2, keepdims=False)
        fine = jnp.zeros((3, spline_base.shape[0], coarse.shape[2]), jnp.float32)
        for tap_index in range(4):
            index = ((spline_base + (tap_index - 1)) % length).astype(jnp.int32)
            taps = jnp.take(coarse, index, axis=1)
            fine = fine + weights[tap_index][None, :, None] * taps
        fine = jnp.transpose(fine, (0, 2, 1))[:, None]
        slab = lax.dynamic_slice_in_dim(padded, layer, 9, 0)
        return scalar_update(slab, fine)[0]

    scalar_segment = lax.map(one_layer, jnp.arange(depth, dtype=jnp.int32))
    return segment, scalar_segment
```

```python
import math

import jax
import jax.numpy as jnp
import numpy as np
from jax import lax
from jax.experimental import pallas as pl
from jax.experimental.pallas import tpu as pltpu
from jax.sharding import PartitionSpec as P

velocity_step = 0.002
viscosity = 0.00125
advect_rate = 0.2
diffuse_rate = 0.05
first_coeffs = (0.8, -0.2, 4.0 / 105.0, -1.0 / 280.0)
second_coeffs = (1.6, -0.2, 8.0 / 315.0, -1.0 / 560.0)
second_centre = -205.0 / 72.0

LENGTH = 1024
GROUP = 32
TILE = 256
f32, bf16 = jnp.float32, jnp.bfloat16


def spectral_tables():
    offset = (np.arange(LENGTH)[None, :] - np.arange(TILE)[:, None]) % LENGTH
    angle = np.pi * offset / LENGTH
    parity = 1.0 - 2.0 * (offset % 2)
    same = offset == 0
    sine = np.where(same, 1.0, np.sin(angle))
    first = np.where(same, 0.0, 0.5 * parity * np.cos(angle) / sine)
    second = np.where(same, -(LENGTH**2) / 12.0 - 1.0 / 6.0, -0.5 * parity / sine**2)
    table = np.concatenate([velocity_step * first, velocity_step * viscosity * second], axis=1)
    high = table.astype(np.float32).astype(jnp.bfloat16)
    low = (table - high.astype(np.float64)).astype(np.float32).astype(jnp.bfloat16)
    return np.concatenate([high, low], axis=1)


def split(value):
    high = value.astype(bf16)
    return high, (value - high.astype(f32)).astype(bf16)


def swap_groups(tiles, lane):
    out = []
    for r in range(4):
        value = tiles[r]
        for c in range(4):
            if c == r:
                continue
            moved = pltpu.roll(tiles[c], (32 * (c - r)) % 128, axis=1)
            value = jnp.where(lane // 32 == c, moved, value)
        out.append(value)
    return out


def shift_lanes(tiles, amount):
    lane = lax.broadcasted_iota(jnp.int32, (8, 128), 1)
    count = len(tiles)
    rolled = [pltpu.roll(tile, amount % 128, axis=1) for tile in tiles]
    if amount > 0:
        return [jnp.where(lane < amount, rolled[i - 1], rolled[i]) for i in range(count)]
    edge = 128 + amount
    return [jnp.where(lane < edge, rolled[i], rolled[(i + 1) % count]) for i in range(count)]


def pack_velocity(vel, send):
    for z in range(8):
        part = vel[pl.ds(z, 96, stride=8), :]
        part = jnp.concatenate([part, jnp.zeros((32, 32), f32)], axis=0)
        send[pl.ds(z, 32, stride=8), :] = part.T


def spectral_segment(recv, table, rows, raw, prod, send):
    lane = lax.broadcasted_iota(jnp.int32, (8, 128), 1)
    totals = [None] * 3
    for x in range(8):
        tiles = [recv[(4 * x + r) * 8 : (4 * x + r) * 8 + 8, :] for r in range(4)]
        got = swap_groups(tiles, lane)
        for c in range(3):
            raw[c, :, 128 * x : 128 * x + 128] = got[c]
            totals[c] = got[c] if x == 0 else totals[c] + got[c]
    for c in range(3):
        mean = jnp.sum(totals[c], axis=1, keepdims=True) * (1.0 / LENGTH)
        for j in range(4):
            rows[j * 24 + c * 8 : j * 24 + c * 8 + 8, :] = (
                raw[c, :, TILE * j : TILE * j + TILE] - mean
            )
    high, low = split(rows[...])
    both = jnp.concatenate([high, low], axis=0)
    for m in range(8):
        cols = slice(TILE * m, TILE * m + TILE)
        lows = slice(2 * LENGTH + TILE * m, 2 * LENGTH + TILE * m + TILE)
        main = jnp.dot(both, table[:, cols], preferred_element_type=f32)
        rest = jnp.dot(high, table[:, lows], preferred_element_type=f32)
        prod[:, cols] = main[:96] + main[96:] + rest
    segment = [[], [], []]
    for k in range(4):
        speed = raw[0, :, TILE * k : TILE * k + TILE]
        for c in range(3):
            first = second = None
            for j in range(4):
                m = (k - j) % 4
                at = slice(j * 24 + c * 8, j * 24 + c * 8 + 8)
                a = prod[at, TILE * m : TILE * m + TILE]
                b = prod[at, LENGTH + TILE * m : LENGTH + TILE * m + TILE]
                first = a if j == 0 else first + a
                second = b if j == 0 else second + b
            own = rows[k * 24 + c * 8 : k * 24 + c * 8 + 8, :]
            value = own + (second - speed * first)
            segment[c] += [value[:, :128], value[:, 128:]]
    within = lane % 32
    halo = [jnp.zeros((8, 128), f32)] * 8
    for c in range(3):
        low_side = shift_lanes(segment[c], 2 + 4 * c)
        high_side = shift_lanes(segment[c], -30 + 4 * c)
        for x in range(8):
            halo[x] = jnp.where(within // 2 == 2 * c, low_side[x], halo[x])
            halo[x] = jnp.where(within // 2 == 2 * c + 1, high_side[x], halo[x])
    for x in range(8):
        tiles = swap_groups([segment[0][x], segment[1][x], segment[2][x], halo[x]], lane)
        for r in range(4):
            send[(4 * x + r) * 8 : (4 * x + r) * 8 + 8, :] = tiles[r]


def spline_matrix(base, frac, first_cell):
    row = lax.broadcasted_iota(jnp.int32, (128, TILE), 0)
    side = row - 96
    halo = side % 4
    slot = jnp.where(row < 96, row % 32 + 2, jnp.where(halo < 2, halo, halo + 32))
    owner = jnp.where(row < 96, row // 32, side // 4)
    local = base - (first_cell - 2)
    square = frac * frac
    cube = square * frac
    weights = (
        (-cube + 2.0 * square - frac) * 0.5,
        (3.0 * cube - 5.0 * square + 2.0) * 0.5,
        (-3.0 * cube + 4.0 * square + frac) * 0.5,
        (cube - square) * 0.5,
    )
    matrix = jnp.zeros((128, TILE), f32)
    for tap in range(4):
        matrix = matrix + jnp.where(slot == local + (tap - 1), weights[tap], 0.0)
    return [jnp.where(owner == c, matrix, 0.0) for c in range(3)]


def pair_sums(window):
    slope = curve = None
    for m in range(1, 5):
        ahead, behind = window(m), window(-m)
        a = first_coeffs[m - 1] * (ahead - behind)
        b = second_coeffs[m - 1] * (ahead + behind)
        slope = a if m == 1 else slope + a
        curve = b if m == 1 else curve + b
    return slope, curve


def stencils(sc, zhalo, ypad, xhalo, slopes, still):
    pad = jnp.zeros((120, TILE), f32)
    left = jnp.concatenate([pad, xhalo[0]], axis=0).T
    right = jnp.concatenate([xhalo[1], pad], axis=0).T
    for z in range(8):
        own = sc[z]

        def along_z(m):
            at = z + m
            if at < 0:
                return zhalo[0, 4 + at]
            return zhalo[1, at - 8] if at >= 8 else sc[at]

        def along_y(m):
            return ypad[z, 8 + m : 40 + m, :]

        wide = jnp.concatenate([left[32 * z : 32 * z + 32], own, right[32 * z : 32 * z + 32]], axis=1)

        def along_x(m):
            return pltpu.roll(wide, (-m) % 512, axis=1)[:, 128:384]

        slope_z, curve_z = pair_sums(along_z)
        slope_y, curve_y = pair_sums(along_y)
        slope_x, curve_x = pair_sums(along_x)
        curve = curve_z + curve_y + curve_x + (3.0 * second_centre) * own
        still[z] = own + diffuse_rate * curve
        slopes[0, z] = advect_rate * slope_x
        slopes[1, z] = advect_rate * slope_y
        slopes[2, z] = advect_rate * slope_z


def finish(recv, weights, slopes, still, lhs, seg_out, sc_out):
    for z in range(8):
        tile = recv[pl.ds(z, 32, stride=8), :]
        lhs[32 * z : 32 * z + 32, :] = tile
        seg_out[pl.ds(z, 96, stride=8), :] = tile.T[:96]
    high, low = split(lhs[...])
    both = jnp.concatenate([high, low], axis=1)
    fine = []
    for c in range(3):
        w_high, w_low = split(weights[c])
        fine.append(
            jnp.dot(both, jnp.concatenate([w_high, w_high], axis=0), preferred_element_type=f32)
            + jnp.dot(high, w_low, preferred_element_type=f32)
        )
    for z in range(8):
        at = slice(32 * z, 32 * z + 32)
        moved = fine[0][at] * slopes[0, z] + fine[1][at] * slopes[1, z] + fine[2][at] * slopes[2, z]
        sc_out[z] = still[z] - moved


def kernel(
    vel_in, sc_in, base_in, frac_in, tab_in, seg_out, sc_out,
    vel, sc, tab, send1, recv1, send2, recv2, rows, raw, prod, lhs,
    zhalo, ysend, yhalo, ypad, xsend, xhalo, slopes, still,
    load_sem, a_send, a_recv, b_send, b_recv, h_send, h_recv,
):
    me = lax.axis_index("blk")
    grp, dep = lax.axis_index("grp"), lax.axis_index("dep")
    n_grp, n_dep = lax.axis_size("grp"), lax.axis_size("dep")

    loads = [
        pltpu.make_async_copy(src, dst, load_sem.at[i])
        for i, (src, dst) in enumerate(((vel_in, vel), (sc_in, sc), (tab_in, tab)))
    ]
    for load in loads:
        load.start()

    barrier = pltpu.get_barrier_semaphore()
    near = (
        {"dep": lax.rem(dep + 1, n_dep)},
        {"dep": lax.rem(dep + n_dep - 1, n_dep)},
        {"grp": lax.rem(grp + 1, n_grp)},
        {"grp": lax.rem(grp + n_grp - 1, n_grp)},
        {"blk": lax.rem(me + 1, GROUP)},
        {"blk": lax.rem(me + GROUP - 1, GROUP)},
    )

    def far_first(j):
        half = (j + 1) // 2
        offset = 16 + half * (2 * lax.rem(j, 2) - 1)
        return lax.rem(me + offset, GROUP)

    def greet(j, carry):
        pl.semaphore_signal(barrier, inc=1, device_id={"blk": far_first(j)}, device_id_type=pl.DeviceIdType.MESH)
        return carry

    lax.fori_loop(0, GROUP - 1, greet, 0)
    for peer in near[:4]:
        pl.semaphore_signal(barrier, inc=1, device_id=peer, device_id_type=pl.DeviceIdType.MESH)

    loads[0].wait()
    pack_velocity(vel, send1)
    loads[1].wait()
    for h in range(2):
        ysend[0, :, 4 * h : 4 * h + 4, :] = sc[4 * h : 4 * h + 4, 28:32, :]
        ysend[1, :, 4 * h : 4 * h + 4, :] = sc[4 * h : 4 * h + 4, 0:4, :]
    flat = sc[...].reshape(TILE, TILE)
    xsend[0] = flat[:, 128:].T[120:]
    xsend[1] = flat[:, :128].T[:8]
    pl.semaphore_wait(barrier, GROUP - 1 + 4)

    def exchange(src, dst, send_sem, recv_sem):
        def step(j, carry):
            peer = far_first(j)
            pltpu.make_async_remote_copy(
                src_ref=src.at[pl.ds(pl.multiple_of(peer * 8, 8), 8)],
                dst_ref=dst.at[pl.ds(pl.multiple_of(me * 8, 8), 8)],
                send_sem=send_sem,
                recv_sem=recv_sem,
                device_id={"blk": peer},
                device_id_type=pl.DeviceIdType.MESH,
            ).start()
            return carry

        lax.fori_loop(0, GROUP - 1, step, 0)
        at = pl.ds(pl.multiple_of(me * 8, 8), 8)
        dst[at, :] = src[at, :]

    def settle(buffer, sem):
        part = buffer.at[pl.ds(0, (GROUP - 1) * 8)]
        pltpu.make_async_copy(part, part, sem).wait()

    exchange(send1, recv1, a_send, a_recv)
    halos = []
    pieces = (
        (sc.at[pl.ds(4, 4)], zhalo.at[0]),
        (sc.at[pl.ds(0, 4)], zhalo.at[1]),
        (ysend.at[0], yhalo.at[0]),
        (ysend.at[1], yhalo.at[1]),
        (xsend.at[0], xhalo.at[0]),
        (xsend.at[1], xhalo.at[1]),
    )
    for i, (src, dst) in enumerate(pieces):
        copy = pltpu.make_async_remote_copy(
            src_ref=src, dst_ref=dst, send_sem=h_send.at[i], recv_sem=h_recv.at[i],
            device_id=near[i], device_id_type=pl.DeviceIdType.MESH,
        )
        copy.start()
        halos.append(copy)
    loads[2].wait()
    settle(recv1, a_recv)
    spectral_segment(recv1, tab, rows, raw, prod, send2)
    exchange(send2, recv2, b_send, b_recv)

    weights = spline_matrix(base_in[...], frac_in[...], me * GROUP)
    for copy in halos:
        copy.wait()
    ypad[:, 8:40, :] = sc[...]
    for h in range(2):
        at = slice(4 * h, 4 * h + 4)
        ypad[at, 4:8, :] = yhalo[0, :, at, :]
        ypad[at, 40:44, :] = yhalo[1, :, at, :]
    stencils(sc, zhalo, ypad, xhalo, slopes, still)
    settle(recv2, b_recv)
    finish(recv2, weights, slopes, still, lhs, seg_out, sc_out)
    settle(send1, a_send)
    settle(send2, b_send)


def per_device(velocity, scalar, spline_base, spline_frac):
    vmem = pl.BlockSpec(memory_space=pltpu.VMEM)
    anywhere = pl.BlockSpec(memory_space=pl.ANY)
    tables = jnp.asarray(spectral_tables())
    segment, out = pl.pallas_call(
        kernel,
        out_shape=(
            jax.ShapeDtypeStruct((768, 32), f32),
            jax.ShapeDtypeStruct((8, 32, TILE), f32),
        ),
        in_specs=[anywhere, anywhere, vmem, vmem, anywhere],
        out_specs=(vmem, vmem),
        scratch_shapes=[
            pltpu.VMEM((768, 32), f32),
            pltpu.VMEM((8, 32, TILE), f32),
            pltpu.VMEM((TILE, 4 * LENGTH), bf16),
            pltpu.VMEM((TILE, 128), f32),
            pltpu.VMEM((TILE, 128), f32),
            pltpu.VMEM((TILE, 128), f32),
            pltpu.VMEM((TILE, 128), f32),
            pltpu.VMEM((96, TILE), f32),
            pltpu.VMEM((3, 8, LENGTH), f32),
            pltpu.VMEM((96, 2 * LENGTH), f32),
            pltpu.VMEM((TILE, 128), f32),
            pltpu.VMEM((2, 4, 32, TILE), f32),
            pltpu.VMEM((2, 4, 8, TILE), f32),
            pltpu.VMEM((2, 4, 8, TILE), f32),
            pltpu.VMEM((8, 48, TILE), f32),
            pltpu.VMEM((2, 8, TILE), f32),
            pltpu.VMEM((2, 8, TILE), f32),
            pltpu.VMEM((3, 8, 32, TILE), f32),
            pltpu.VMEM((8, 32, TILE), f32),
            pltpu.SemaphoreType.DMA((3,)),
            pltpu.SemaphoreType.DMA,
            pltpu.SemaphoreType.DMA,
            pltpu.SemaphoreType.DMA,
            pltpu.SemaphoreType.DMA,
            pltpu.SemaphoreType.DMA((6,)),
            pltpu.SemaphoreType.DMA((6,)),
        ],
        compiler_params=pltpu.CompilerParams(collective_id=0, has_side_effects=True),
        name="segment",
    )(
        velocity.reshape(768, 32),
        scalar,
        spline_base.reshape(1, TILE),
        spline_frac.reshape(1, TILE),
        tables,
    )
    return segment.reshape(velocity.shape), out


def solution(mesh):
    in_specs = (P(None, "blk", "dep", "grp"), P("dep", "grp", "blk"), P("blk"), P("blk"))
    out_specs = (P(None, "blk", "dep", "grp"), P("dep", "grp", "blk"))
    return jax.shard_map(
        per_device, mesh=mesh, in_specs=in_specs, out_specs=out_specs, check_vma=False
    )
```

```python
import math

import jax
import jax.numpy as jnp
import numpy as np
from jax import lax
from jax.experimental import pallas as pl
from jax.experimental.pallas import tpu as pltpu
from jax.sharding import PartitionSpec as P

velocity_step = 0.002
viscosity = 0.00125
advect_rate = 0.2
diffuse_rate = 0.05
first_coeffs = (0.8, -0.2, 4.0 / 105.0, -1.0 / 280.0)
second_coeffs = (1.6, -0.2, 8.0 / 315.0, -1.0 / 560.0)
second_centre = -205.0 / 72.0

LENGTH = 1024
GROUP = 32
TILE = 256
f32, bf16 = jnp.float32, jnp.bfloat16


def spectral_tables():
    offset = (np.arange(LENGTH)[None, :] - np.arange(TILE)[:, None]) % LENGTH
    angle = np.pi * offset / LENGTH
    parity = 1.0 - 2.0 * (offset % 2)
    same = offset == 0
    sine = np.where(same, 1.0, np.sin(angle))
    first = np.where(same, 0.0, 0.5 * parity * np.cos(angle) / sine)
    second = np.where(same, -(LENGTH**2) / 12.0 - 1.0 / 6.0, -0.5 * parity / sine**2)
    table = np.concatenate([velocity_step * first, velocity_step * viscosity * second], axis=1)
    high = table.astype(np.float32).astype(jnp.bfloat16)
    low = (table - high.astype(np.float64)).astype(np.float32).astype(jnp.bfloat16)
    return np.concatenate([high, low], axis=1)


def split(value):
    high = value.astype(bf16)
    return high, (value - high.astype(f32)).astype(bf16)


def swap_groups(tiles, lane):
    out = []
    for r in range(4):
        value = tiles[r]
        for c in range(4):
            if c == r:
                continue
            moved = pltpu.roll(tiles[c], (32 * (c - r)) % 128, axis=1)
            value = jnp.where(lane // 32 == c, moved, value)
        out.append(value)
    return out


def shift_lanes(tiles, amount):
    lane = lax.broadcasted_iota(jnp.int32, (8, 128), 1)
    count = len(tiles)
    rolled = [pltpu.roll(tile, amount % 128, axis=1) for tile in tiles]
    if amount > 0:
        return [jnp.where(lane < amount, rolled[i - 1], rolled[i]) for i in range(count)]
    edge = 128 + amount
    return [jnp.where(lane < edge, rolled[i], rolled[(i + 1) % count]) for i in range(count)]


def pack_velocity(vel, send):
    for z in range(8):
        part = vel[pl.ds(z, 96, stride=8), :]
        part = jnp.concatenate([part, jnp.zeros((32, 32), f32)], axis=0)
        send[pl.ds(z, 32, stride=8), :] = part.T


def spectral_segment(recv, table, rows, raw, prod, send):
    lane = lax.broadcasted_iota(jnp.int32, (8, 128), 1)
    totals = [[None] * 3, [None] * 3]
    for y in range(2):
        own = slice(8 * y, 8 * y + 8)
        for x in range(8):
            tiles = [recv[(4 * x + r) * 16 + 8 * y : (4 * x + r) * 16 + 8 * y + 8, :] for r in range(4)]
            got = swap_groups(tiles, lane)
            for c in range(3):
                raw[c, own, 128 * x : 128 * x + 128] = got[c]
                totals[y][c] = got[c] if x == 0 else totals[y][c] + got[c]
    for y in range(2):
        own = slice(8 * y, 8 * y + 8)
        for c in range(3):
            mean = jnp.sum(totals[y][c], axis=1, keepdims=True) * (1.0 / LENGTH)
            for j in range(4):
                at = j * 48 + c * 16 + 8 * y
                rows[at : at + 8, :] = raw[c, own, TILE * j : TILE * j + TILE] - mean
    high, low = split(rows[...])
    both = jnp.concatenate([high, low], axis=0)
    for m in range(8):
        cols = slice(TILE * m, TILE * m + TILE)
        lows = slice(2 * LENGTH + TILE * m, 2 * LENGTH + TILE * m + TILE)
        main = jnp.dot(both, table[:, cols], preferred_element_type=f32)
        rest = jnp.dot(high, table[:, lows], preferred_element_type=f32)
        prod[:, cols] = main[:192] + main[192:] + rest
    within = lane % 32
    for y in range(2):
        segment = [[], [], []]
        for k in range(4):
            speed = raw[0, 8 * y : 8 * y + 8, TILE * k : TILE * k + TILE]
            for c in range(3):
                first = second = None
                for j in range(4):
                    m = (k - j) % 4
                    at = slice(j * 48 + c * 16 + 8 * y, j * 48 + c * 16 + 8 * y + 8)
                    a = prod[at, TILE * m : TILE * m + TILE]
                    b = prod[at, LENGTH + TILE * m : LENGTH + TILE * m + TILE]
                    first = a if j == 0 else first + a
                    second = b if j == 0 else second + b
                at = k * 48 + c * 16 + 8 * y
                value = rows[at : at + 8, :] + (second - speed * first)
                segment[c] += [value[:, :128], value[:, 128:]]
        halo = [jnp.zeros((8, 128), f32)] * 8
        for c in range(3):
            low_side = shift_lanes(segment[c], 2 + 4 * c)
            high_side = shift_lanes(segment[c], -30 + 4 * c)
            for x in range(8):
                halo[x] = jnp.where(within // 2 == 2 * c, low_side[x], halo[x])
                halo[x] = jnp.where(within // 2 == 2 * c + 1, high_side[x], halo[x])
        for x in range(8):
            tiles = swap_groups([segment[0][x], segment[1][x], segment[2][x], halo[x]], lane)
            for r in range(4):
                at = (4 * x + r) * 16 + 8 * y
                send[at : at + 8, :] = tiles[r]


def spline_matrix(base, frac, first_cell):
    row = lax.broadcasted_iota(jnp.int32, (128, TILE), 0)
    side = row - 96
    halo = side % 4
    slot = jnp.where(row < 96, row % 32 + 2, jnp.where(halo < 2, halo, halo + 32))
    owner = jnp.where(row < 96, row // 32, side // 4)
    local = base - (first_cell - 2)
    square = frac * frac
    cube = square * frac
    weights = (
        (-cube + 2.0 * square - frac) * 0.5,
        (3.0 * cube - 5.0 * square + 2.0) * 0.5,
        (-3.0 * cube + 4.0 * square + frac) * 0.5,
        (cube - square) * 0.5,
    )
    matrix = jnp.zeros((128, TILE), f32)
    for tap in range(4):
        matrix = matrix + jnp.where(slot == local + (tap - 1), weights[tap], 0.0)
    return [jnp.where(owner == c, matrix, 0.0) for c in range(3)]


def pair_sums(window):
    slope = curve = None
    for m in range(1, 5):
        ahead, behind = window(m), window(-m)
        a = first_coeffs[m - 1] * (ahead - behind)
        b = second_coeffs[m - 1] * (ahead + behind)
        slope = a if m == 1 else slope + a
        curve = b if m == 1 else curve + b
    return slope, curve


def stencils(sc, zhalo, ypad, xhalo, slopes, still):
    pad = jnp.zeros((120, TILE), f32)
    left = jnp.concatenate([pad, xhalo[0]], axis=0).T
    right = jnp.concatenate([xhalo[1], pad], axis=0).T
    for z in range(8):
        own = sc[z]

        def along_z(m):
            at = z + m
            if at < 0:
                return zhalo[0, 4 + at]
            return zhalo[1, at - 8] if at >= 8 else sc[at]

        def along_y(m):
            return ypad[z, 8 + m : 40 + m, :]

        wide = jnp.concatenate([left[32 * z : 32 * z + 32], own, right[32 * z : 32 * z + 32]], axis=1)

        def along_x(m):
            return pltpu.roll(wide, (-m) % 512, axis=1)[:, 128:384]

        slope_z, curve_z = pair_sums(along_z)
        slope_y, curve_y = pair_sums(along_y)
        slope_x, curve_x = pair_sums(along_x)
        curve = curve_z + curve_y + curve_x + (3.0 * second_centre) * own
        still[z] = own + diffuse_rate * curve
        slopes[0, z] = advect_rate * slope_x
        slopes[1, z] = advect_rate * slope_y
        slopes[2, z] = advect_rate * slope_z


def tail(tiles, weights, slopes, still, seg_out, sc_out, lhs):
    for z in range(8):
        tile = tiles[pl.ds(z, 32, stride=8), :]
        lhs[32 * z : 32 * z + 32, :] = tile
        seg_out[pl.ds(z, 96, stride=8), :] = tile.T[:96]
    high, low = split(lhs[...])
    both = jnp.concatenate([high, low], axis=1)
    fine = []
    for c in range(3):
        w_high, w_low = split(weights[c])
        fine.append(
            jnp.dot(both, jnp.concatenate([w_high, w_high], axis=0), preferred_element_type=f32)
            + jnp.dot(high, w_low, preferred_element_type=f32)
        )
    for z in range(8):
        at = slice(32 * z, 32 * z + 32)
        moved = fine[0][at] * slopes[0, z] + fine[1][at] * slopes[1, z] + fine[2][at] * slopes[2, z]
        sc_out[z] = still[z] - moved


def kernel(
    vel_in, sc_in, base_in, frac_in, tab_in, tiles_out, weights_out, slopes, still,
    vel, sc, tab, base, frac, send1, recv1, send2, recv2, rows, raw, prod,
    zhalo, ysend, yhalo, ypad, xsend, xhalo,
    load_sem, a_send, a_recv, b_send, b_recv, h_send, h_recv,
):
    me = lax.axis_index("blk")
    grp, dep = lax.axis_index("grp"), lax.axis_index("dep")
    n_grp, n_dep = lax.axis_size("grp"), lax.axis_size("dep")
    owner = lax.rem(me, 2)
    owns = owner == 1
    mesh_id = pl.DeviceIdType.MESH

    loads = [
        pltpu.make_async_copy(src, dst, load_sem.at[i])
        for i, (src, dst) in enumerate(
            ((vel_in, vel), (sc_in, sc), (tab_in, tab), (base_in, base), (frac_in, frac))
        )
    ]
    for load in loads:
        load.start()

    barrier = pltpu.get_barrier_semaphore()
    near = (
        {"dep": lax.rem(dep + 1, n_dep)},
        {"dep": lax.rem(dep + n_dep - 1, n_dep)},
        {"grp": lax.rem(grp + 1, n_grp)},
        {"grp": lax.rem(grp + n_grp - 1, n_grp)},
        {"blk": lax.rem(me + 1, GROUP)},
        {"blk": lax.rem(me + GROUP - 1, GROUP)},
    )
    z_first, y_first, x_first = lax.rem(dep, 2), 1 - lax.rem(grp, 2), 1 - owner

    def around(j, half):
        return half + ((j + 1) // 2) * (2 * lax.rem(j, 2) - 1)

    def peer_of(j):
        return lax.rem(me + around(j, 16), GROUP)

    def owner_of(j):
        return lax.rem(me // 2 + around(j, 8), 16)

    def greet(j, carry):
        pl.semaphore_signal(barrier, inc=1, device_id={"blk": peer_of(j)}, device_id_type=mesh_id)
        return carry

    lax.fori_loop(0, owner * (GROUP - 1), greet, 0)
    for first, at in ((z_first, 0), (y_first, 2)):

        @pl.when(first == 0)
        def _():
            for peer in near[at : at + 2]:
                pl.semaphore_signal(barrier, inc=1, device_id=peer, device_id_type=mesh_id)

    loads[0].wait()
    pack_velocity(vel, send1)
    pl.semaphore_wait(barrier, 16 - owner + 2 * z_first + 2 * y_first)

    def piece(buffer, index):
        return buffer.at[pl.ds(pl.multiple_of(index * 16, 16), 16)]

    def to_owner(j, carry):
        index = owner_of(j)
        pltpu.make_async_remote_copy(
            src_ref=piece(send1, index), dst_ref=piece(recv1, me), send_sem=a_send, recv_sem=a_recv,
            device_id={"blk": 2 * index + 1}, device_id_type=mesh_id,
        ).start()
        return carry

    def to_peer(j, carry):
        peer = peer_of(j)
        pltpu.make_async_remote_copy(
            src_ref=piece(send2, peer), dst_ref=piece(recv2, me // 2), send_sem=b_send, recv_sem=b_recv,
            device_id={"blk": peer}, device_id_type=mesh_id,
        ).start()
        return carry

    def settle(buffer, count, sem):
        part = buffer.at[pl.ds(0, 16 * count)]
        pltpu.make_async_copy(part, part, sem).wait()

    lax.fori_loop(0, 16 - owner, to_owner, 0)

    loads[1].wait()
    for h in range(2):
        ysend[0, :, 4 * h : 4 * h + 4, :] = sc[4 * h : 4 * h + 4, 28:32, :]
        ysend[1, :, 4 * h : 4 * h + 4, :] = sc[4 * h : 4 * h + 4, 0:4, :]
    flat = sc[...].reshape(TILE, TILE)
    xsend[0] = flat[:, 128:].T[120:]
    xsend[1] = flat[:, :128].T[:8]
    pieces = (
        (sc.at[pl.ds(4, 4)], zhalo.at[0]),
        (sc.at[pl.ds(0, 4)], zhalo.at[1]),
        (ysend.at[0], yhalo.at[0]),
        (ysend.at[1], yhalo.at[1]),
        (xsend.at[0], xhalo.at[0]),
        (xsend.at[1], xhalo.at[1]),
    )
    halos = [
        pltpu.make_async_remote_copy(
            src_ref=src, dst_ref=dst, send_sem=h_send.at[i], recv_sem=h_recv.at[i],
            device_id=near[i], device_id_type=mesh_id,
        )
        for i, (src, dst) in enumerate(pieces)
    ]
    sides = ((x_first, halos[4:6]), (y_first, halos[2:4]), (z_first, halos[0:2]))
    for first, pair in sides:

        @pl.when(first == 1)
        def _():
            for copy in pair:
                copy.start()

    loads[2].wait()

    @pl.when(owns)
    def _():
        recv1[pl.ds(pl.multiple_of(me * 16, 16), 16), :] = send1[pl.ds(pl.multiple_of(me // 2 * 16, 16), 16), :]
        settle(recv1, GROUP - 1, a_recv)
        spectral_segment(recv1, tab, rows, raw, prod, send2)
        lax.fori_loop(0, GROUP - 1, to_peer, 0)
        recv2[pl.ds(pl.multiple_of(me // 2 * 16, 16), 16), :] = send2[pl.ds(pl.multiple_of(me * 16, 16), 16), :]

    loads[3].wait()
    loads[4].wait()
    spline = spline_matrix(base[...], frac[...], me * GROUP)
    for c in range(3):
        weights_out[c] = spline[c]
    for first, pair in sides:

        @pl.when(first == 0)
        def _():
            for copy in pair:
                copy.wait_recv()
            for copy in pair:
                copy.start()

    for first, pair in sides:

        @pl.when(first == 1)
        def _():
            for copy in pair:
                copy.wait_recv()

    ypad[:, 8:40, :] = sc[...]
    for h in range(2):
        at = slice(4 * h, 4 * h + 4)
        ypad[at, 4:8, :] = yhalo[0, :, at, :]
        ypad[at, 40:44, :] = yhalo[1, :, at, :]
    stencils(sc, zhalo, ypad, xhalo, slopes, still)

    @pl.when(owns)
    def _():
        settle(recv2, 15, b_recv)
        settle(send1, 15, a_send)
        settle(send2, GROUP - 1, b_send)

    @pl.when(jnp.logical_not(owns))
    def _():
        settle(recv2, 16, b_recv)
        settle(send1, 16, a_send)

    tiles_out[...] = recv2[...]
    for copy in halos:
        copy.wait_send()


def per_device(velocity, scalar, spline_base, spline_frac):
    vmem = pl.BlockSpec(memory_space=pltpu.VMEM)
    hbm = pl.BlockSpec(memory_space=pltpu.HBM)
    tables = jnp.asarray(spectral_tables())
    parts = pl.pallas_call(
        kernel,
        out_shape=(
            jax.ShapeDtypeStruct((TILE, 128), f32),
            jax.ShapeDtypeStruct((3, 128, TILE), f32),
            jax.ShapeDtypeStruct((3, 8, 32, TILE), f32),
            jax.ShapeDtypeStruct((8, 32, TILE), f32),
        ),
        in_specs=[hbm] * 5,
        out_specs=(vmem,) * 4,
        scratch_shapes=[
            pltpu.VMEM((768, 32), f32),
            pltpu.VMEM((8, 32, TILE), f32),
            pltpu.VMEM((TILE, 4 * LENGTH), bf16),
            pltpu.VMEM((1, TILE), jnp.int32),
            pltpu.VMEM((1, TILE), f32),
            pltpu.VMEM((TILE, 128), f32),
            pltpu.VMEM((2 * TILE, 128), f32),
            pltpu.VMEM((2 * TILE, 128), f32),
            pltpu.VMEM((TILE, 128), f32),
            pltpu.VMEM((192, TILE), f32),
            pltpu.VMEM((3, 16, LENGTH), f32),
            pltpu.VMEM((192, 2 * LENGTH), f32),
            pltpu.VMEM((2, 4, 32, TILE), f32),
            pltpu.VMEM((2, 4, 8, TILE), f32),
            pltpu.VMEM((2, 4, 8, TILE), f32),
            pltpu.VMEM((8, 48, TILE), f32),
            pltpu.VMEM((2, 8, TILE), f32),
            pltpu.VMEM((2, 8, TILE), f32),
            pltpu.SemaphoreType.DMA((5,)),
            pltpu.SemaphoreType.DMA,
            pltpu.SemaphoreType.DMA,
            pltpu.SemaphoreType.DMA,
            pltpu.SemaphoreType.DMA,
            pltpu.SemaphoreType.DMA((6,)),
            pltpu.SemaphoreType.DMA((6,)),
        ],
        compiler_params=pltpu.CompilerParams(
            collective_id=0, has_side_effects=True, vmem_limit_bytes=24 * 2**20
        ),
        name="segment",
    )(
        *(
            pltpu.with_memory_space_constraint(x, pltpu.HBM)
            for x in (
                velocity.reshape(768, 32),
                scalar,
                spline_base.reshape(1, TILE),
                spline_frac.reshape(1, TILE),
                tables,
            )
        )
    )
    segment, out = pl.pallas_call(
        tail,
        out_shape=(
            jax.ShapeDtypeStruct((768, 32), f32),
            jax.ShapeDtypeStruct((8, 32, TILE), f32),
        ),
        in_specs=[vmem] * 4,
        out_specs=(vmem, vmem),
        scratch_shapes=[pltpu.VMEM((TILE, 128), f32)],
        compiler_params=pltpu.CompilerParams(vmem_limit_bytes=24 * 2**20),
        name="tail",
    )(*parts)
    return segment.reshape(velocity.shape), out


def solution(mesh):
    in_specs = (P(None, "blk", "dep", "grp"), P("dep", "grp", "blk"), P("blk"), P("blk"))
    out_specs = (P(None, "blk", "dep", "grp"), P("dep", "grp", "blk"))
    return jax.shard_map(
        per_device, mesh=mesh, in_specs=in_specs, out_specs=out_specs, check_vma=False
    )
```

```python
import math

import jax
import jax.numpy as jnp
import numpy as np
from jax import lax
from jax.experimental import pallas as pl
from jax.experimental.pallas import tpu as pltpu
from jax.sharding import PartitionSpec as P

velocity_step = 0.002
viscosity = 0.00125
advect_rate = 0.2
diffuse_rate = 0.05
first_coeffs = (0.8, -0.2, 4.0 / 105.0, -1.0 / 280.0)
second_coeffs = (1.6, -0.2, 8.0 / 315.0, -1.0 / 560.0)
second_centre = -205.0 / 72.0

LENGTH = 1024
GROUP = 32
TILE = 256
f32, bf16 = jnp.float32, jnp.bfloat16


def spectral_tables():
    offset = (np.arange(LENGTH)[None, :] - np.arange(TILE)[:, None]) % LENGTH
    angle = np.pi * offset / LENGTH
    parity = 1.0 - 2.0 * (offset % 2)
    same = offset == 0
    sine = np.where(same, 1.0, np.sin(angle))
    first = np.where(same, 0.0, 0.5 * parity * np.cos(angle) / sine)
    second = np.where(same, -(LENGTH**2) / 12.0 - 1.0 / 6.0, -0.5 * parity / sine**2)
    table = np.concatenate([velocity_step * first, velocity_step * viscosity * second], axis=1)
    high = table.astype(np.float32).astype(jnp.bfloat16)
    low = (table - high.astype(np.float64)).astype(np.float32).astype(jnp.bfloat16)
    return np.concatenate([high, low], axis=1)


def split(value):
    high = value.astype(bf16)
    return high, (value - high.astype(f32)).astype(bf16)


def swap_groups(tiles, lane):
    out = []
    for r in range(4):
        value = tiles[r]
        for c in range(4):
            if c == r:
                continue
            moved = pltpu.roll(tiles[c], (32 * (c - r)) % 128, axis=1)
            value = jnp.where(lane // 32 == c, moved, value)
        out.append(value)
    return out


def shift_lanes(tiles, amount):
    lane = lax.broadcasted_iota(jnp.int32, (8, 128), 1)
    count = len(tiles)
    rolled = [pltpu.roll(tile, amount % 128, axis=1) for tile in tiles]
    if amount > 0:
        return [jnp.where(lane < amount, rolled[i - 1], rolled[i]) for i in range(count)]
    edge = 128 + amount
    return [jnp.where(lane < edge, rolled[i], rolled[(i + 1) % count]) for i in range(count)]


def pack_velocity(vel, send):
    for z in range(8):
        part = vel[pl.ds(z, 96, stride=8), :]
        part = jnp.concatenate([part, jnp.zeros((32, 32), f32)], axis=0)
        send[pl.ds(z, 32, stride=8), :] = part.T


def spectral_segment(recv, table, rows, raw, prod, send):
    lane = lax.broadcasted_iota(jnp.int32, (8, 128), 1)
    totals = [[None] * 3, [None] * 3]
    for y in range(2):
        own = slice(8 * y, 8 * y + 8)
        for x in range(8):
            tiles = [recv[(4 * x + r) * 16 + 8 * y : (4 * x + r) * 16 + 8 * y + 8, :] for r in range(4)]
            got = swap_groups(tiles, lane)
            for c in range(3):
                raw[c, own, 128 * x : 128 * x + 128] = got[c]
                totals[y][c] = got[c] if x == 0 else totals[y][c] + got[c]
    for y in range(2):
        own = slice(8 * y, 8 * y + 8)
        for c in range(3):
            mean = jnp.sum(totals[y][c], axis=1, keepdims=True) * (1.0 / LENGTH)
            for j in range(4):
                at = j * 48 + c * 16 + 8 * y
                rows[at : at + 8, :] = raw[c, own, TILE * j : TILE * j + TILE] - mean
    high, low = split(rows[...])
    both = jnp.concatenate([high, low], axis=0)
    for m in range(8):
        cols = slice(TILE * m, TILE * m + TILE)
        lows = slice(2 * LENGTH + TILE * m, 2 * LENGTH + TILE * m + TILE)
        main = jnp.dot(both, table[:, cols], preferred_element_type=f32)
        rest = jnp.dot(high, table[:, lows], preferred_element_type=f32)
        prod[:, cols] = main[:192] + main[192:] + rest
    within = lane % 32
    for y in range(2):
        segment = [[], [], []]
        for k in range(4):
            speed = raw[0, 8 * y : 8 * y + 8, TILE * k : TILE * k + TILE]
            for c in range(3):
                first = second = None
                for j in range(4):
                    m = (k - j) % 4
                    at = slice(j * 48 + c * 16 + 8 * y, j * 48 + c * 16 + 8 * y + 8)
                    a = prod[at, TILE * m : TILE * m + TILE]
                    b = prod[at, LENGTH + TILE * m : LENGTH + TILE * m + TILE]
                    first = a if j == 0 else first + a
                    second = b if j == 0 else second + b
                at = k * 48 + c * 16 + 8 * y
                value = rows[at : at + 8, :] + (second - speed * first)
                segment[c] += [value[:, :128], value[:, 128:]]
        halo = [jnp.zeros((8, 128), f32)] * 8
        for c in range(3):
            low_side = shift_lanes(segment[c], 2 + 4 * c)
            high_side = shift_lanes(segment[c], -30 + 4 * c)
            for x in range(8):
                halo[x] = jnp.where(within // 2 == 2 * c, low_side[x], halo[x])
                halo[x] = jnp.where(within // 2 == 2 * c + 1, high_side[x], halo[x])
        for x in range(8):
            tiles = swap_groups([segment[0][x], segment[1][x], segment[2][x], halo[x]], lane)
            for r in range(4):
                at = (4 * x + r) * 16 + 8 * y
                send[at : at + 8, :] = tiles[r]


def spline_matrix(base, frac, first_cell):
    row = lax.broadcasted_iota(jnp.int32, (128, TILE), 0)
    side = row - 96
    halo = side % 4
    slot = jnp.where(row < 96, row % 32 + 2, jnp.where(halo < 2, halo, halo + 32))
    owner = jnp.where(row < 96, row // 32, side // 4)
    local = base - (first_cell - 2)
    square = frac * frac
    cube = square * frac
    weights = (
        (-cube + 2.0 * square - frac) * 0.5,
        (3.0 * cube - 5.0 * square + 2.0) * 0.5,
        (-3.0 * cube + 4.0 * square + frac) * 0.5,
        (cube - square) * 0.5,
    )
    matrix = jnp.zeros((128, TILE), f32)
    for tap in range(4):
        matrix = matrix + jnp.where(slot == local + (tap - 1), weights[tap], 0.0)
    return [jnp.where(owner == c, matrix, 0.0) for c in range(3)]


def pair_sums(window):
    slope = curve = None
    for m in range(1, 5):
        ahead, behind = window(m), window(-m)
        a = first_coeffs[m - 1] * (ahead - behind)
        b = second_coeffs[m - 1] * (ahead + behind)
        slope = a if m == 1 else slope + a
        curve = b if m == 1 else curve + b
    return slope, curve


def stencils_xy(sc, ypad, xhalo, slopes, still):
    pad = jnp.zeros((120, TILE), f32)
    left = jnp.concatenate([pad, xhalo[0]], axis=0).T
    right = jnp.concatenate([xhalo[1], pad], axis=0).T
    for z in range(8):
        own = sc[z]

        def along_y(m):
            return ypad[z, 8 + m : 40 + m, :]

        wide = jnp.concatenate([left[32 * z : 32 * z + 32], own, right[32 * z : 32 * z + 32]], axis=1)

        def along_x(m):
            return pltpu.roll(wide, (-m) % 512, axis=1)[:, 128:384]

        slope_y, curve_y = pair_sums(along_y)
        slope_x, curve_x = pair_sums(along_x)
        curve = curve_y + curve_x + (3.0 * second_centre) * own
        still[z] = own + diffuse_rate * curve
        slopes[0, z] = advect_rate * slope_x
        slopes[1, z] = advect_rate * slope_y


def stencils_z(sc, zhalo, slopes, still):
    for z in range(8):

        def along_z(m):
            at = z + m
            if at < 0:
                return zhalo[0, 4 + at]
            return zhalo[1, at - 8] if at >= 8 else sc[at]

        slope_z, curve_z = pair_sums(along_z)
        still[z] = still[z] + diffuse_rate * curve_z
        slopes[2, z] = advect_rate * slope_z


def tail(tiles, weights, slopes, still, seg_out, sc_out, lhs):
    for z in range(8):
        tile = tiles[pl.ds(z, 32, stride=8), :]
        lhs[32 * z : 32 * z + 32, :] = tile
        seg_out[pl.ds(z, 96, stride=8), :] = tile.T[:96]
    high, low = split(lhs[...])
    both = jnp.concatenate([high, low], axis=1)
    fine = []
    for c in range(3):
        w_high, w_low = split(weights[c])
        fine.append(
            jnp.dot(both, jnp.concatenate([w_high, w_high], axis=0), preferred_element_type=f32)
            + jnp.dot(high, w_low, preferred_element_type=f32)
        )
    for z in range(8):
        at = slice(32 * z, 32 * z + 32)
        moved = fine[0][at] * slopes[0, z] + fine[1][at] * slopes[1, z] + fine[2][at] * slopes[2, z]
        sc_out[z] = still[z] - moved


def kernel(
    vel_in, sc_in, base_in, frac_in, tab_in, tiles_out, weights_out, slopes, still,
    vel, sc, tab, base, frac, send1, recv1, send2, recv2, rows, raw, prod,
    zhalo, ysend, yhalo, ypad, xsend, xhalo,
    load_sem, a_send, a_recv, b_send, b_recv, h_send, h_recv, hello, go, met,
):
    me = lax.axis_index("blk")
    grp, dep = lax.axis_index("grp"), lax.axis_index("dep")
    n_grp, n_dep = lax.axis_size("grp"), lax.axis_size("dep")
    mesh_id = pl.DeviceIdType.MESH
    x, rest = me // 4, lax.rem(me, 4)
    owner = x // 6 + lax.rem((x + 1) // 2, 2) * (1 - x // 4)
    owns, guest = owner == 1, owner == 0
    mine = (x - 1 - 3 * (x // 6)) * 4 + rest
    host = ((x // 3) * (1 - x // 4) + (x - 2) * (x // 4)) * 4 + rest

    def owner_at(index):
        return (index // 4 + 1 + 3 * (index // 8)) * 4 + lax.rem(index, 4)

    def cube(bit):
        size = 2**bit
        return {"blk": owner_at(mine + size * (1 - 2 * lax.rem(mine // size, 2)))}

    def guest_at():
        q = mine // 4
        return {"blk": (3 * q * (1 - q // 2) + (q + 2) * (q // 2)) * 4 + rest}

    def signal(sem, peer):
        pl.semaphore_signal(sem, inc=1, device_id=peer, device_id_type=mesh_id)

    loads = [
        pltpu.make_async_copy(src, dst, load_sem.at[i])
        for i, (src, dst) in enumerate(
            ((vel_in, vel), (sc_in, sc), (tab_in, tab), (base_in, base), (frac_in, frac))
        )
    ]
    for i in (0, 1, 3, 4):
        loads[i].start()

    barrier = pltpu.get_barrier_semaphore()
    near = (
        {"dep": lax.rem(dep + 1, n_dep)},
        {"dep": lax.rem(dep + n_dep - 1, n_dep)},
        {"grp": lax.rem(grp + 1, n_grp)},
        {"grp": lax.rem(grp + n_grp - 1, n_grp)},
        {"blk": lax.rem(me + 1, GROUP)},
        {"blk": lax.rem(me + GROUP - 1, GROUP)},
    )
    up, down = dep // (n_dep - 1), (dep + n_dep - 1) // n_dep
    high, middle = grp // 2, lax.rem((grp + 1) // 2, 2)
    turned = (dep + n_dep - 1) // n_dep
    ahead = 1 - lax.rem(me, 2) + turned * (me // (GROUP - 1))
    behind = 1 - lax.rem(me, 2) - turned * ((GROUP - me) // GROUP)
    first = (up, down, high, middle, ahead, behind)
    for i in range(6):

        @pl.when(first[i] == 0)
        def _():
            signal(barrier, near[i])

    def greet(j, carry):
        signal(barrier, {"blk": j + (j - me + GROUP) // GROUP})
        return carry

    lax.fori_loop(0, owner * (1 - up) * (GROUP - 1), greet, 0)

    @pl.when(owner * up == 1)
    def _():
        signal(barrier, guest_at())
        for bit in range(4):
            signal(barrier, cube(bit))

    expected = (1 - up) * (16 - owner) + up * (1 + 3 * owner)
    pl.semaphore_wait(barrier, expected + up + down + high + middle + ahead + behind)

    pieces = (
        (sc_in.at[pl.ds(4, 4)], zhalo.at[0]),
        (sc_in.at[pl.ds(0, 4)], zhalo.at[1]),
        (ysend.at[0], yhalo.at[0]),
        (ysend.at[1], yhalo.at[1]),
        (xsend.at[0], xhalo.at[0]),
        (xsend.at[1], xhalo.at[1]),
    )
    halos = [
        pltpu.make_async_remote_copy(
            src_ref=src, dst_ref=dst, send_sem=h_send.at[i], recv_sem=h_recv.at[i],
            device_id=near[i], device_id_type=mesh_id,
        )
        for i, (src, dst) in enumerate(pieces)
    ]

    def send_first(indices):
        for i in indices:

            @pl.when(first[i] == 1)
            def _():
                halos[i].start()

    def reply(indices):
        for i in indices:

            @pl.when(first[i] == 0)
            def _():
                halos[i ^ 1].wait_recv()
                halos[i].start()

    def receive(indices):
        for i in indices:

            @pl.when(first[i] == 1)
            def _():
                halos[i ^ 1].wait_recv()

    def piece(buffer, index):
        return buffer.at[pl.ds(pl.multiple_of(index * 16, 16), 16)]

    def to_owner(start):
        def step(j, carry):
            index = lax.rem(start + j, 16)
            pltpu.make_async_remote_copy(
                src_ref=piece(send1, index), dst_ref=piece(recv1, me), send_sem=a_send, recv_sem=a_recv,
                device_id={"blk": owner_at(index)}, device_id_type=mesh_id,
            ).start()
            return carry

        return step

    def to_peer(j, carry):
        peer = j + (j - me + GROUP) // GROUP
        pltpu.make_async_remote_copy(
            src_ref=piece(send2, peer), dst_ref=piece(recv2, mine), send_sem=b_send, recv_sem=b_recv,
            device_id={"blk": peer}, device_id_type=mesh_id,
        ).start()
        return carry

    def settle(buffer, count, sem):
        part = buffer.at[pl.ds(0, 16 * count)]
        pltpu.make_async_copy(part, part, sem).wait()

    @pl.when((1 - owner) * up == 1)
    def _():
        signal(hello, {"blk": owner_at(host)})

    @pl.when(owner * up == 1)
    def _():
        signal(met.at[0], cube(0))

    send_first((0, 1))
    loads[0].wait()
    pack_velocity(vel, send1)

    @pl.when((1 - owner) * up == 1)
    def _():
        pl.semaphore_wait(go, 1)

    @pl.when(owner * up == 1)
    def _():
        for bit in range(4):
            pl.semaphore_wait(met.at[bit], 1)
            if bit < 3:
                signal(met.at[bit + 1], cube(bit + 1))

    lax.fori_loop(0, 16 - owner, to_owner(owner * (mine + 1) + 4 * (1 - owner)), 0)

    @pl.when(owner * up == 1)
    def _():
        pl.semaphore_wait(hello, 1)
        signal(go, guest_at())

    @pl.when(owns)
    def _():
        loads[2].start()

    loads[1].wait()
    for h in range(2):
        ysend[0, :, 4 * h : 4 * h + 4, :] = sc[4 * h : 4 * h + 4, 28:32, :]
        ysend[1, :, 4 * h : 4 * h + 4, :] = sc[4 * h : 4 * h + 4, 0:4, :]
    flat = sc[...].reshape(TILE, TILE)
    xsend[0] = flat[:, 128:].T[120:]
    xsend[1] = flat[:, :128].T[:8]
    send_first((4, 5, 2, 3))
    reply((4, 5))

    @pl.when(owns)
    def _():
        loads[2].wait()
        recv1[pl.ds(pl.multiple_of(me * 16, 16), 16), :] = send1[pl.ds(pl.multiple_of(mine * 16, 16), 16), :]
        settle(recv1, GROUP - 1, a_recv)
        spectral_segment(recv1, tab, rows, raw, prod, send2)
        lax.fori_loop(0, GROUP - 1, to_peer, 0)
        recv2[pl.ds(pl.multiple_of(mine * 16, 16), 16), :] = send2[pl.ds(pl.multiple_of(me * 16, 16), 16), :]

    reply((2, 3, 0))
    loads[3].wait()
    loads[4].wait()
    spline = spline_matrix(base[...], frac[...], me * GROUP)
    for c in range(3):
        weights_out[c] = spline[c]
    receive((4, 5, 2, 3))
    ypad[:, 8:40, :] = sc[...]
    for h in range(2):
        at = slice(4 * h, 4 * h + 4)
        ypad[at, 4:8, :] = yhalo[0, :, at, :]
        ypad[at, 40:44, :] = yhalo[1, :, at, :]
    stencils_xy(sc, ypad, xhalo, slopes, still)
    reply((1,))
    receive((0, 1))
    stencils_z(sc, zhalo, slopes, still)

    @pl.when(owns)
    def _():
        settle(recv2, 15, b_recv)
        settle(send1, 15, a_send)
        settle(send2, GROUP - 1, b_send)

    @pl.when(guest)
    def _():
        settle(recv2, 16, b_recv)
        settle(send1, 16, a_send)

    tiles_out[...] = recv2[...]
    for copy in halos:
        copy.wait_send()


def per_device(velocity, scalar, spline_base, spline_frac):
    vmem = pl.BlockSpec(memory_space=pltpu.VMEM)
    hbm = pl.BlockSpec(memory_space=pltpu.HBM)
    tables = jnp.asarray(spectral_tables())
    parts = pl.pallas_call(
        kernel,
        out_shape=(
            jax.ShapeDtypeStruct((TILE, 128), f32),
            jax.ShapeDtypeStruct((3, 128, TILE), f32),
            jax.ShapeDtypeStruct((3, 8, 32, TILE), f32),
            jax.ShapeDtypeStruct((8, 32, TILE), f32),
        ),
        in_specs=[hbm] * 5,
        out_specs=(vmem,) * 4,
        scratch_shapes=[
            pltpu.VMEM((768, 32), f32),
            pltpu.VMEM((8, 32, TILE), f32),
            pltpu.VMEM((TILE, 4 * LENGTH), bf16),
            pltpu.VMEM((1, TILE), jnp.int32),
            pltpu.VMEM((1, TILE), f32),
            pltpu.VMEM((TILE, 128), f32),
            pltpu.VMEM((2 * TILE, 128), f32),
            pltpu.VMEM((2 * TILE, 128), f32),
            pltpu.VMEM((TILE, 128), f32),
            pltpu.VMEM((192, TILE), f32),
            pltpu.VMEM((3, 16, LENGTH), f32),
            pltpu.VMEM((192, 2 * LENGTH), f32),
            pltpu.VMEM((2, 4, 32, TILE), f32),
            pltpu.VMEM((2, 4, 8, TILE), f32),
            pltpu.VMEM((2, 4, 8, TILE), f32),
            pltpu.VMEM((8, 48, TILE), f32),
            pltpu.VMEM((2, 8, TILE), f32),
            pltpu.VMEM((2, 8, TILE), f32),
            pltpu.SemaphoreType.DMA((5,)),
            pltpu.SemaphoreType.DMA,
            pltpu.SemaphoreType.DMA,
            pltpu.SemaphoreType.DMA,
            pltpu.SemaphoreType.DMA,
            pltpu.SemaphoreType.DMA((6,)),
            pltpu.SemaphoreType.DMA((6,)),
            pltpu.SemaphoreType.REGULAR,
            pltpu.SemaphoreType.REGULAR,
            pltpu.SemaphoreType.REGULAR((4,)),
        ],
        compiler_params=pltpu.CompilerParams(
            collective_id=0, has_side_effects=True, vmem_limit_bytes=24 * 2**20
        ),
        name="segment",
    )(
        *(
            pltpu.with_memory_space_constraint(x, pltpu.HBM)
            for x in (
                velocity.reshape(768, 32),
                scalar,
                spline_base.reshape(1, TILE),
                spline_frac.reshape(1, TILE),
                tables,
            )
        )
    )
    segment, out = pl.pallas_call(
        tail,
        out_shape=(
            jax.ShapeDtypeStruct((768, 32), f32),
            jax.ShapeDtypeStruct((8, 32, TILE), f32),
        ),
        in_specs=[vmem] * 4,
        out_specs=(vmem, vmem),
        scratch_shapes=[pltpu.VMEM((TILE, 128), f32)],
        compiler_params=pltpu.CompilerParams(vmem_limit_bytes=24 * 2**20),
        name="tail",
    )(*parts)
    return segment.reshape(velocity.shape), out


def solution(mesh):
    in_specs = (P(None, "blk", "dep", "grp"), P("dep", "grp", "blk"), P("blk"), P("blk"))
    out_specs = (P(None, "blk", "dep", "grp"), P("dep", "grp", "blk"))
    return jax.shard_map(
        per_device, mesh=mesh, in_specs=in_specs, out_specs=out_specs, check_vma=False
    )
```

```python
import math

import jax
import jax.numpy as jnp
import numpy as np
from jax import lax
from jax.experimental import pallas as pl
from jax.experimental.pallas import tpu as pltpu
from jax.sharding import PartitionSpec as P

velocity_step = 0.002
viscosity = 0.00125
advect_rate = 0.2
diffuse_rate = 0.05
first_coeffs = (0.8, -0.2, 4.0 / 105.0, -1.0 / 280.0)
second_coeffs = (1.6, -0.2, 8.0 / 315.0, -1.0 / 560.0)
second_centre = -205.0 / 72.0

LENGTH = 1024
GROUP = 32
TILE = 256
f32, bf16 = jnp.float32, jnp.bfloat16


def spectral_tables():
    offset = (np.arange(LENGTH)[None, :] - np.arange(TILE)[:, None]) % LENGTH
    angle = np.pi * offset / LENGTH
    parity = 1.0 - 2.0 * (offset % 2)
    same = offset == 0
    sine = np.where(same, 1.0, np.sin(angle))
    first = np.where(same, 0.0, 0.5 * parity * np.cos(angle) / sine)
    second = np.where(same, -(LENGTH**2) / 12.0 - 1.0 / 6.0, -0.5 * parity / sine**2)
    table = np.concatenate([velocity_step * first, velocity_step * viscosity * second], axis=1)
    high = table.astype(np.float32).astype(jnp.bfloat16)
    low = (table - high.astype(np.float64)).astype(np.float32).astype(jnp.bfloat16)
    return np.concatenate([high, low], axis=1)


def split(value):
    high = value.astype(bf16)
    return high, (value - high.astype(f32)).astype(bf16)


def swap_groups(tiles, lane):
    out = []
    for r in range(4):
        value = tiles[r]
        for c in range(4):
            if c == r:
                continue
            moved = pltpu.roll(tiles[c], (32 * (c - r)) % 128, axis=1)
            value = jnp.where(lane // 32 == c, moved, value)
        out.append(value)
    return out


def shift_lanes(tiles, amount):
    lane = lax.broadcasted_iota(jnp.int32, (8, 128), 1)
    count = len(tiles)
    rolled = [pltpu.roll(tile, amount % 128, axis=1) for tile in tiles]
    if amount > 0:
        return [jnp.where(lane < amount, rolled[i - 1], rolled[i]) for i in range(count)]
    edge = 128 + amount
    return [jnp.where(lane < edge, rolled[i], rolled[(i + 1) % count]) for i in range(count)]


def pack_velocity(vel, send):
    for z in range(8):
        part = vel[pl.ds(z, 96, stride=8), :]
        part = jnp.concatenate([part, jnp.zeros((32, 32), f32)], axis=0)
        send[pl.ds(z, 32, stride=8), :] = part.T


def spectral_segment(recv, table, rows, raw, prod, send, dispatch):
    lane = lax.broadcasted_iota(jnp.int32, (8, 128), 1)
    totals = [[None] * 3, [None] * 3]
    for y in range(2):
        own = slice(8 * y, 8 * y + 8)
        for x in range(8):
            tiles = [recv[(4 * x + r) * 16 + 8 * y : (4 * x + r) * 16 + 8 * y + 8, :] for r in range(4)]
            got = swap_groups(tiles, lane)
            for c in range(3):
                raw[c, own, 128 * x : 128 * x + 128] = got[c]
                totals[y][c] = got[c] if x == 0 else totals[y][c] + got[c]
    for y in range(2):
        own = slice(8 * y, 8 * y + 8)
        for c in range(3):
            mean = jnp.sum(totals[y][c], axis=1, keepdims=True) * (1.0 / LENGTH)
            for j in range(4):
                at = j * 48 + c * 16 + 8 * y
                rows[at : at + 8, :] = raw[c, own, TILE * j : TILE * j + TILE] - mean
    high, low = split(rows[...])
    both = jnp.concatenate([high, low], axis=0)
    for m in range(8):
        cols = slice(TILE * m, TILE * m + TILE)
        lows = slice(2 * LENGTH + TILE * m, 2 * LENGTH + TILE * m + TILE)
        main = jnp.dot(both, table[:, cols], preferred_element_type=f32)
        rest = jnp.dot(high, table[:, lows], preferred_element_type=f32)
        prod[:, cols] = main[:192] + main[192:] + rest
    within = lane % 32
    packed = []
    for y in range(2):
        segment = [[], [], []]
        for k in range(4):
            speed = raw[0, 8 * y : 8 * y + 8, TILE * k : TILE * k + TILE]
            for c in range(3):
                first = second = None
                for j in range(4):
                    m = (k - j) % 4
                    at = slice(j * 48 + c * 16 + 8 * y, j * 48 + c * 16 + 8 * y + 8)
                    a = prod[at, TILE * m : TILE * m + TILE]
                    b = prod[at, LENGTH + TILE * m : LENGTH + TILE * m + TILE]
                    first = a if j == 0 else first + a
                    second = b if j == 0 else second + b
                at = k * 48 + c * 16 + 8 * y
                value = rows[at : at + 8, :] + (second - speed * first)
                segment[c] += [value[:, :128], value[:, 128:]]
        halo = [jnp.zeros((8, 128), f32)] * 8
        for c in range(3):
            low_side = shift_lanes(segment[c], 2 + 4 * c)
            high_side = shift_lanes(segment[c], -30 + 4 * c)
            for x in range(8):
                halo[x] = jnp.where(within // 2 == 2 * c, low_side[x], halo[x])
                halo[x] = jnp.where(within // 2 == 2 * c + 1, high_side[x], halo[x])
        packed.append(segment + [halo])
    for x in range(8):
        for y in range(2):
            tiles = swap_groups([packed[y][c][x] for c in range(4)], lane)
            for r in range(4):
                at = (4 * x + r) * 16 + 8 * y
                send[at : at + 8, :] = tiles[r]
        if x > 0:
            dispatch(x - 1)
    dispatch(7)


def spline_matrix(base, frac, first_cell):
    row = lax.broadcasted_iota(jnp.int32, (128, TILE), 0)
    side = row - 96
    halo = side % 4
    slot = jnp.where(row < 96, row % 32 + 2, jnp.where(halo < 2, halo, halo + 32))
    owner = jnp.where(row < 96, row // 32, side // 4)
    local = base - (first_cell - 2)
    square = frac * frac
    cube = square * frac
    weights = (
        (-cube + 2.0 * square - frac) * 0.5,
        (3.0 * cube - 5.0 * square + 2.0) * 0.5,
        (-3.0 * cube + 4.0 * square + frac) * 0.5,
        (cube - square) * 0.5,
    )
    matrix = jnp.zeros((128, TILE), f32)
    for tap in range(4):
        matrix = matrix + jnp.where(slot == local + (tap - 1), weights[tap], 0.0)
    return [jnp.where(owner == c, matrix, 0.0) for c in range(3)]


def pair_sums(window):
    slope = curve = None
    for m in range(1, 5):
        ahead, behind = window(m), window(-m)
        a = first_coeffs[m - 1] * (ahead - behind)
        b = second_coeffs[m - 1] * (ahead + behind)
        slope = a if m == 1 else slope + a
        curve = b if m == 1 else curve + b
    return slope, curve


def stencils_xy(sc, ypad, xhalo, slopes, still):
    pad = jnp.zeros((120, TILE), f32)
    left = jnp.concatenate([pad, xhalo[0]], axis=0).T
    right = jnp.concatenate([xhalo[1], pad], axis=0).T
    for z in range(8):
        own = sc[z]

        def along_y(m):
            return ypad[z, 8 + m : 40 + m, :]

        wide = jnp.concatenate([left[32 * z : 32 * z + 32], own, right[32 * z : 32 * z + 32]], axis=1)

        def along_x(m):
            return pltpu.roll(wide, (-m) % 512, axis=1)[:, 128:384]

        slope_y, curve_y = pair_sums(along_y)
        slope_x, curve_x = pair_sums(along_x)
        curve = curve_y + curve_x + (3.0 * second_centre) * own
        still[z] = own + diffuse_rate * curve
        slopes[0, z] = advect_rate * slope_x
        slopes[1, z] = advect_rate * slope_y


def stencils_z(sc, zhalo, slopes, still):
    for z in range(8):

        def along_z(m):
            at = z + m
            if at < 0:
                return zhalo[0, 4 + at]
            return zhalo[1, at - 8] if at >= 8 else sc[at]

        slope_z, curve_z = pair_sums(along_z)
        still[z] = still[z] + diffuse_rate * curve_z
        slopes[2, z] = advect_rate * slope_z


def tail(tiles, weights, slopes, still, seg_out, sc_out, lhs, seg, sc, sems):
    for z in range(8):
        tile = tiles[pl.ds(z, 32, stride=8), :]
        lhs[32 * z : 32 * z + 32, :] = tile
        seg[pl.ds(z, 96, stride=8), :] = tile.T[:96]
    high, low = split(lhs[...])
    both = jnp.concatenate([high, low], axis=1)
    copies = [pltpu.make_async_copy(seg, seg_out, sems.at[0])]
    copies[0].start()
    fine = []
    for c in range(3):
        w_high, w_low = split(weights[c])
        fine.append(
            jnp.dot(both, jnp.concatenate([w_high, w_high], axis=0), preferred_element_type=f32)
            + jnp.dot(high, w_low, preferred_element_type=f32)
        )
    for z in range(8):
        at = slice(32 * z, 32 * z + 32)
        moved = fine[0][at] * slopes[0, z] + fine[1][at] * slopes[1, z] + fine[2][at] * slopes[2, z]
        sc[z] = still[z] - moved
        if z % 4 == 3:
            half = pl.ds(z - 3, 4)
            copies.append(pltpu.make_async_copy(sc.at[half], sc_out.at[half], sems.at[1 + z // 4]))
            copies[-1].start()
    for copy in copies:
        copy.wait()


def kernel(
    vel_in, sc_in, base_in, frac_in, tab_in, tiles_out, weights_out, slopes, still,
    vel, sc, tab, base, frac, send1, recv1, send2, recv2, rows, raw, prod,
    zhalo, ysend, yhalo, ypad, xsend, xhalo,
    load_sem, a_send, a_recv, b_send, b_recv, h_send, h_recv, hello, go, met,
):
    me = lax.axis_index("blk")
    grp, dep = lax.axis_index("grp"), lax.axis_index("dep")
    n_grp, n_dep = lax.axis_size("grp"), lax.axis_size("dep")
    mesh_id = pl.DeviceIdType.MESH
    x, rest = me // 4, lax.rem(me, 4)
    owner = lax.rem(x, 2)
    owns, guest = owner == 1, owner == 0
    mine = x // 2 * 4 + rest
    host = x // 2 * 4 + rest

    def owner_at(index):
        return (index // 4 * 2 + 1) * 4 + lax.rem(index, 4)

    def cube(bit):
        if bit == 3:
            return {"blk": owner_at(mine + 4 * (3 - 2 * (mine // 4)))}
        size = 2**bit
        return {"blk": owner_at(mine + size * (1 - 2 * lax.rem(mine // size, 2)))}

    def guest_at():
        return {"blk": me - 4}

    def signal(sem, peer):
        pl.semaphore_signal(sem, inc=1, device_id=peer, device_id_type=mesh_id)

    loads = [
        pltpu.make_async_copy(src, dst, load_sem.at[i])
        for i, (src, dst) in enumerate(
            ((vel_in, vel), (sc_in, sc), (tab_in, tab), (base_in, base), (frac_in, frac))
        )
    ]
    for i in (0, 1, 3, 4):
        loads[i].start()

    barrier = pltpu.get_barrier_semaphore()
    near = (
        {"dep": lax.rem(dep + 1, n_dep)},
        {"dep": lax.rem(dep + n_dep - 1, n_dep)},
        {"grp": lax.rem(grp + 1, n_grp)},
        {"grp": lax.rem(grp + n_grp - 1, n_grp)},
        {"blk": lax.rem(me + 1, GROUP)},
        {"blk": lax.rem(me + GROUP - 1, GROUP)},
    )
    up, down = dep // (n_dep - 1), (dep + n_dep - 1) // n_dep
    high, middle = grp // 2, lax.rem((grp + 1) // 2, 2)
    turned = (dep + n_dep - 1) // n_dep
    ahead = 1 - lax.rem(me, 2) + turned * (me // (GROUP - 1))
    behind = 1 - lax.rem(me, 2) - turned * ((GROUP - me) // GROUP)
    first = (up, down, high, middle, ahead, behind)
    for i in range(6):

        @pl.when(first[i] == 0)
        def _():
            signal(barrier, near[i])

    def greet(j, carry):
        signal(barrier, {"blk": j + (j - me + GROUP) // GROUP})
        return carry

    lax.fori_loop(0, owner * (1 - up) * (GROUP - 1), greet, 0)

    @pl.when(owner * up == 1)
    def _():
        signal(barrier, guest_at())
        for bit in range(4):
            signal(barrier, cube(bit))

    expected = (1 - up) * (16 - owner) + up * (1 + 3 * owner)
    pl.semaphore_wait(barrier, expected + up + down + high + middle + ahead + behind)

    pieces = (
        (sc_in.at[pl.ds(4, 4)], zhalo.at[0]),
        (sc_in.at[pl.ds(0, 4)], zhalo.at[1]),
        (ysend.at[0], yhalo.at[0]),
        (ysend.at[1], yhalo.at[1]),
        (xsend.at[0], xhalo.at[0]),
        (xsend.at[1], xhalo.at[1]),
    )
    halos = [
        pltpu.make_async_remote_copy(
            src_ref=src, dst_ref=dst, send_sem=h_send.at[i], recv_sem=h_recv.at[i],
            device_id=near[i], device_id_type=mesh_id,
        )
        for i, (src, dst) in enumerate(pieces)
    ]

    def send_first(indices):
        for i in indices:

            @pl.when(first[i] == 1)
            def _():
                halos[i].start()

    def reply(indices):
        for i in indices:

            @pl.when(first[i] == 0)
            def _():
                halos[i ^ 1].wait_recv()
                halos[i].start()

    def receive(indices):
        for i in indices:

            @pl.when(first[i] == 1)
            def _():
                halos[i ^ 1].wait_recv()

    def piece(buffer, index):
        start = index * 16 if isinstance(index, int) else pl.multiple_of(index * 16, 16)
        return buffer.at[pl.ds(start, 16)]

    def to_owner(start):
        def step(j, carry):
            index = lax.rem(start + j, 16)
            pltpu.make_async_remote_copy(
                src_ref=piece(send1, index), dst_ref=piece(recv1, me), send_sem=a_send, recv_sem=a_recv,
                device_id={"blk": owner_at(index)}, device_id_type=mesh_id,
            ).start()
            return carry

        return step

    def to_column(column):
        for r in range(4):
            peer = 4 * column + r

            @pl.when(me != peer)
            def _():
                pltpu.make_async_remote_copy(
                    src_ref=piece(send2, peer), dst_ref=piece(recv2, mine), send_sem=b_send, recv_sem=b_recv,
                    device_id={"blk": peer}, device_id_type=mesh_id,
                ).start()

    def settle(buffer, count, sem):
        part = buffer.at[pl.ds(0, 16 * count)]
        pltpu.make_async_copy(part, part, sem).wait()

    @pl.when((1 - owner) * up == 1)
    def _():
        signal(hello, {"blk": owner_at(host)})

    @pl.when(owner * up == 1)
    def _():
        signal(met.at[0], cube(0))

    send_first((0, 1))
    loads[0].wait()
    pack_velocity(vel, send1)

    @pl.when((1 - owner) * up == 1)
    def _():
        pl.semaphore_wait(go, 1)

    @pl.when(owner * up == 1)
    def _():
        for bit in range(4):
            pl.semaphore_wait(met.at[bit], 1)
            if bit < 3:
                signal(met.at[bit + 1], cube(bit + 1))

    lax.fori_loop(0, 16 - owner, to_owner(owner * (mine + 1) + 4 * (1 - owner)), 0)

    @pl.when(owner * up == 1)
    def _():
        pl.semaphore_wait(hello, 1)
        signal(go, guest_at())

    @pl.when(owns)
    def _():
        loads[2].start()

    loads[1].wait()
    for h in range(2):
        ysend[0, :, 4 * h : 4 * h + 4, :] = sc[4 * h : 4 * h + 4, 28:32, :]
        ysend[1, :, 4 * h : 4 * h + 4, :] = sc[4 * h : 4 * h + 4, 0:4, :]
    flat = sc[...].reshape(TILE, TILE)
    xsend[0] = flat[:, 128:].T[120:]
    xsend[1] = flat[:, :128].T[:8]
    send_first((4, 5, 2, 3))
    reply((4, 5))

    @pl.when(owns)
    def _():
        loads[2].wait()
        recv1[pl.ds(pl.multiple_of(me * 16, 16), 16), :] = send1[pl.ds(pl.multiple_of(mine * 16, 16), 16), :]
        settle(recv1, GROUP - 1, a_recv)
        spectral_segment(recv1, tab, rows, raw, prod, send2, to_column)
        recv2[pl.ds(pl.multiple_of(mine * 16, 16), 16), :] = send2[pl.ds(pl.multiple_of(me * 16, 16), 16), :]

    reply((2, 3, 0))
    loads[3].wait()
    loads[4].wait()
    spline = spline_matrix(base[...], frac[...], me * GROUP)
    for c in range(3):
        weights_out[c] = spline[c]
    receive((4, 5, 2, 3))
    ypad[:, 8:40, :] = sc[...]
    for h in range(2):
        at = slice(4 * h, 4 * h + 4)
        ypad[at, 4:8, :] = yhalo[0, :, at, :]
        ypad[at, 40:44, :] = yhalo[1, :, at, :]
    stencils_xy(sc, ypad, xhalo, slopes, still)
    reply((1,))
    receive((0, 1))
    stencils_z(sc, zhalo, slopes, still)

    @pl.when(owns)
    def _():
        settle(recv2, 15, b_recv)
        settle(send1, 15, a_send)
        settle(send2, GROUP - 1, b_send)

    @pl.when(guest)
    def _():
        settle(recv2, 16, b_recv)
        settle(send1, 16, a_send)

    tiles_out[...] = recv2[...]
    for copy in halos:
        copy.wait_send()


def per_device(velocity, scalar, spline_base, spline_frac):
    vmem = pl.BlockSpec(memory_space=pltpu.VMEM)
    hbm = pl.BlockSpec(memory_space=pltpu.HBM)
    tables = jnp.asarray(spectral_tables())
    parts = pl.pallas_call(
        kernel,
        out_shape=(
            jax.ShapeDtypeStruct((TILE, 128), f32),
            jax.ShapeDtypeStruct((3, 128, TILE), f32),
            jax.ShapeDtypeStruct((3, 8, 32, TILE), f32),
            jax.ShapeDtypeStruct((8, 32, TILE), f32),
        ),
        in_specs=[hbm] * 5,
        out_specs=(vmem,) * 4,
        scratch_shapes=[
            pltpu.VMEM((768, 32), f32),
            pltpu.VMEM((8, 32, TILE), f32),
            pltpu.VMEM((TILE, 4 * LENGTH), bf16),
            pltpu.VMEM((1, TILE), jnp.int32),
            pltpu.VMEM((1, TILE), f32),
            pltpu.VMEM((TILE, 128), f32),
            pltpu.VMEM((2 * TILE, 128), f32),
            pltpu.VMEM((2 * TILE, 128), f32),
            pltpu.VMEM((TILE, 128), f32),
            pltpu.VMEM((192, TILE), f32),
            pltpu.VMEM((3, 16, LENGTH), f32),
            pltpu.VMEM((192, 2 * LENGTH), f32),
            pltpu.VMEM((2, 4, 32, TILE), f32),
            pltpu.VMEM((2, 4, 8, TILE), f32),
            pltpu.VMEM((2, 4, 8, TILE), f32),
            pltpu.VMEM((8, 48, TILE), f32),
            pltpu.VMEM((2, 8, TILE), f32),
            pltpu.VMEM((2, 8, TILE), f32),
            pltpu.SemaphoreType.DMA((5,)),
            pltpu.SemaphoreType.DMA,
            pltpu.SemaphoreType.DMA,
            pltpu.SemaphoreType.DMA,
            pltpu.SemaphoreType.DMA,
            pltpu.SemaphoreType.DMA((6,)),
            pltpu.SemaphoreType.DMA((6,)),
            pltpu.SemaphoreType.REGULAR,
            pltpu.SemaphoreType.REGULAR,
            pltpu.SemaphoreType.REGULAR((4,)),
        ],
        compiler_params=pltpu.CompilerParams(
            collective_id=0, has_side_effects=True, vmem_limit_bytes=24 * 2**20
        ),
        name="segment",
    )(
        *(
            pltpu.with_memory_space_constraint(x, pltpu.HBM)
            for x in (
                velocity.reshape(768, 32),
                scalar,
                spline_base.reshape(1, TILE),
                spline_frac.reshape(1, TILE),
                tables,
            )
        )
    )
    segment, out = pl.pallas_call(
        tail,
        out_shape=(
            jax.ShapeDtypeStruct((768, 32), f32),
            jax.ShapeDtypeStruct((8, 32, TILE), f32),
        ),
        in_specs=[vmem] * 4,
        out_specs=(hbm, hbm),
        scratch_shapes=[
            pltpu.VMEM((TILE, 128), f32),
            pltpu.VMEM((768, 32), f32),
            pltpu.VMEM((8, 32, TILE), f32),
            pltpu.SemaphoreType.DMA((3,)),
        ],
        compiler_params=pltpu.CompilerParams(vmem_limit_bytes=24 * 2**20),
        name="tail",
    )(*parts)
    return segment.reshape(velocity.shape), out


def solution(mesh):
    in_specs = (P(None, "blk", "dep", "grp"), P("dep", "grp", "blk"), P("blk"), P("blk"))
    out_specs = (P(None, "blk", "dep", "grp"), P("dep", "grp", "blk"))
    return jax.shard_map(
        per_device, mesh=mesh, in_specs=in_specs, out_specs=out_specs, check_vma=False
    )
```

```python
import math

import jax
import jax.numpy as jnp
import numpy as np
from jax import lax
from jax.experimental import pallas as pl
from jax.experimental.pallas import tpu as pltpu
from jax.sharding import PartitionSpec as P

velocity_step = 0.002
viscosity = 0.00125
advect_rate = 0.2
diffuse_rate = 0.05
first_coeffs = (0.8, -0.2, 4.0 / 105.0, -1.0 / 280.0)
second_coeffs = (1.6, -0.2, 8.0 / 315.0, -1.0 / 560.0)
second_centre = -205.0 / 72.0

LENGTH = 1024
GROUP = 32
TILE = 256
f32, bf16 = jnp.float32, jnp.bfloat16


def spectral_tables():
    offset = (np.arange(LENGTH)[None, :] - np.arange(TILE)[:, None]) % LENGTH
    angle = np.pi * offset / LENGTH
    parity = 1.0 - 2.0 * (offset % 2)
    same = offset == 0
    sine = np.where(same, 1.0, np.sin(angle))
    first = np.where(same, 0.0, 0.5 * parity * np.cos(angle) / sine)
    second = np.where(same, -(LENGTH**2) / 12.0 - 1.0 / 6.0, -0.5 * parity / sine**2)
    table = np.concatenate([velocity_step * first, velocity_step * viscosity * second], axis=1)
    high = table.astype(np.float32).astype(jnp.bfloat16)
    low = (table - high.astype(np.float64)).astype(np.float32).astype(jnp.bfloat16)
    return np.concatenate([high, low], axis=1)


def split(value):
    high = value.astype(bf16)
    return high, (value - high.astype(f32)).astype(bf16)


def swap_groups(tiles, lane):
    out = []
    for r in range(4):
        value = tiles[r]
        for c in range(4):
            if c == r:
                continue
            moved = pltpu.roll(tiles[c], (32 * (c - r)) % 128, axis=1)
            value = jnp.where(lane // 32 == c, moved, value)
        out.append(value)
    return out


def shift_lanes(tiles, amount):
    lane = lax.broadcasted_iota(jnp.int32, (8, 128), 1)
    count = len(tiles)
    rolled = [pltpu.roll(tile, amount % 128, axis=1) for tile in tiles]
    if amount > 0:
        return [jnp.where(lane < amount, rolled[i - 1], rolled[i]) for i in range(count)]
    edge = 128 + amount
    return [jnp.where(lane < edge, rolled[i], rolled[(i + 1) % count]) for i in range(count)]


def pack_velocity(vel, send):
    for z in range(8):
        part = vel[pl.ds(z, 96, stride=8), :]
        part = jnp.concatenate([part, jnp.zeros((32, 32), f32)], axis=0)
        send[pl.ds(z, 32, stride=8), :] = part.T


def spectral_segment(recv, table, rows, raw, prod, send, dispatch):
    lane = lax.broadcasted_iota(jnp.int32, (8, 128), 1)
    totals = [[None] * 3, [None] * 3]
    for y in range(2):
        own = slice(8 * y, 8 * y + 8)
        for x in range(8):
            tiles = [recv[(4 * x + r) * 16 + 8 * y : (4 * x + r) * 16 + 8 * y + 8, :] for r in range(4)]
            got = swap_groups(tiles, lane)
            for c in range(3):
                raw[c, own, 128 * x : 128 * x + 128] = got[c]
                totals[y][c] = got[c] if x == 0 else totals[y][c] + got[c]
    for y in range(2):
        own = slice(8 * y, 8 * y + 8)
        for c in range(3):
            mean = jnp.sum(totals[y][c], axis=1, keepdims=True) * (1.0 / LENGTH)
            for j in range(4):
                at = j * 48 + c * 16 + 8 * y
                rows[at : at + 8, :] = raw[c, own, TILE * j : TILE * j + TILE] - mean
    high, low = split(rows[...])
    both = jnp.concatenate([high, low], axis=0)
    for m in range(8):
        cols = slice(TILE * m, TILE * m + TILE)
        lows = slice(2 * LENGTH + TILE * m, 2 * LENGTH + TILE * m + TILE)
        main = jnp.dot(both, table[:, cols], preferred_element_type=f32)
        rest = jnp.dot(high, table[:, lows], preferred_element_type=f32)
        prod[:, cols] = main[:192] + main[192:] + rest
    within = lane % 32
    packed = []
    for y in range(2):
        segment = [[], [], []]
        for k in range(4):
            speed = raw[0, 8 * y : 8 * y + 8, TILE * k : TILE * k + TILE]
            for c in range(3):
                first = second = None
                for j in range(4):
                    m = (k - j) % 4
                    at = slice(j * 48 + c * 16 + 8 * y, j * 48 + c * 16 + 8 * y + 8)
                    a = prod[at, TILE * m : TILE * m + TILE]
                    b = prod[at, LENGTH + TILE * m : LENGTH + TILE * m + TILE]
                    first = a if j == 0 else first + a
                    second = b if j == 0 else second + b
                at = k * 48 + c * 16 + 8 * y
                value = rows[at : at + 8, :] + (second - speed * first)
                segment[c] += [value[:, :128], value[:, 128:]]
        halo = [jnp.zeros((8, 128), f32)] * 8
        for c in range(3):
            low_side = shift_lanes(segment[c], 2 + 4 * c)
            high_side = shift_lanes(segment[c], -30 + 4 * c)
            for x in range(8):
                halo[x] = jnp.where(within // 2 == 2 * c, low_side[x], halo[x])
                halo[x] = jnp.where(within // 2 == 2 * c + 1, high_side[x], halo[x])
        packed.append(segment + [halo])
    order = (0, 1, 7, 2, 6, 3, 5, 4)
    for i, x in enumerate(order):
        for y in range(2):
            tiles = swap_groups([packed[y][c][x] for c in range(4)], lane)
            for r in range(4):
                at = (4 * x + r) * 16 + 8 * y
                send[at : at + 8, :] = tiles[r]
        if i > 0:
            dispatch(order[i - 1])
    dispatch(order[-1])


def spline_matrix(base, frac, first_cell):
    row = lax.broadcasted_iota(jnp.int32, (128, TILE), 0)
    side = row - 96
    halo = side % 4
    slot = jnp.where(row < 96, row % 32 + 2, jnp.where(halo < 2, halo, halo + 32))
    owner = jnp.where(row < 96, row // 32, side // 4)
    local = base - (first_cell - 2)
    square = frac * frac
    cube = square * frac
    weights = (
        (-cube + 2.0 * square - frac) * 0.5,
        (3.0 * cube - 5.0 * square + 2.0) * 0.5,
        (-3.0 * cube + 4.0 * square + frac) * 0.5,
        (cube - square) * 0.5,
    )
    matrix = jnp.zeros((128, TILE), f32)
    for tap in range(4):
        matrix = matrix + jnp.where(slot == local + (tap - 1), weights[tap], 0.0)
    return [jnp.where(owner == c, matrix, 0.0) for c in range(3)]


def pair_sums(window):
    slope = curve = None
    for m in range(1, 5):
        ahead, behind = window(m), window(-m)
        a = first_coeffs[m - 1] * (ahead - behind)
        b = second_coeffs[m - 1] * (ahead + behind)
        slope = a if m == 1 else slope + a
        curve = b if m == 1 else curve + b
    return slope, curve


def stencils_xy(sc, ypad, xhalo, slopes, still):
    pad = jnp.zeros((120, TILE), f32)
    left = jnp.concatenate([pad, xhalo[0]], axis=0).T
    right = jnp.concatenate([xhalo[1], pad], axis=0).T
    for z in range(8):
        own = sc[z]

        def along_y(m):
            return ypad[z, 8 + m : 40 + m, :]

        wide = jnp.concatenate([left[32 * z : 32 * z + 32], own, right[32 * z : 32 * z + 32]], axis=1)

        def along_x(m):
            return pltpu.roll(wide, (-m) % 512, axis=1)[:, 128:384]

        slope_y, curve_y = pair_sums(along_y)
        slope_x, curve_x = pair_sums(along_x)
        curve = curve_y + curve_x + (3.0 * second_centre) * own
        still[z] = own + diffuse_rate * curve
        slopes[0, z] = advect_rate * slope_x
        slopes[1, z] = advect_rate * slope_y


def stencils_z(sc, zhalo, slopes, still):
    for z in range(8):

        def along_z(m):
            at = z + m
            if at < 0:
                return zhalo[0, 4 + at]
            return zhalo[1, at - 8] if at >= 8 else sc[at]

        slope_z, curve_z = pair_sums(along_z)
        still[z] = still[z] + diffuse_rate * curve_z
        slopes[2, z] = advect_rate * slope_z


def tail(tiles, weights, slopes, still, seg_out, sc_out, lhs, seg, sc, sems):
    for z in range(8):
        tile = tiles[pl.ds(z, 32, stride=8), :]
        lhs[32 * z : 32 * z + 32, :] = tile
        seg[pl.ds(z, 96, stride=8), :] = tile.T[:96]
    high, low = split(lhs[...])
    both = jnp.concatenate([high, low], axis=1)
    copies = [pltpu.make_async_copy(seg, seg_out, sems.at[0])]
    copies[0].start()
    fine = []
    for c in range(3):
        w_high, w_low = split(weights[c])
        fine.append(
            jnp.dot(both, jnp.concatenate([w_high, w_high], axis=0), preferred_element_type=f32)
            + jnp.dot(high, w_low, preferred_element_type=f32)
        )
    for z in range(8):
        at = slice(32 * z, 32 * z + 32)
        moved = fine[0][at] * slopes[0, z] + fine[1][at] * slopes[1, z] + fine[2][at] * slopes[2, z]
        sc[z] = still[z] - moved
        if z % 4 == 3:
            half = pl.ds(z - 3, 4)
            copies.append(pltpu.make_async_copy(sc.at[half], sc_out.at[half], sems.at[1 + z // 4]))
            copies[-1].start()
    for copy in copies:
        copy.wait()


def kernel(
    vel_in, sc_in, base_in, frac_in, tab_in, tiles_out, weights_out, slopes, still,
    vel, sc, tab, base, frac, send1, recv1, send2, recv2, rows, raw, prod,
    zhalo, ysend, yhalo, ypad, xsend, xhalo,
    load_sem, a_send, a_recv, b_send, b_recv, h_send, h_recv, hello, go, met,
):
    me = lax.axis_index("blk")
    grp, dep = lax.axis_index("grp"), lax.axis_index("dep")
    n_grp, n_dep = lax.axis_size("grp"), lax.axis_size("dep")
    mesh_id = pl.DeviceIdType.MESH
    x, rest = me // 4, lax.rem(me, 4)
    owner = lax.rem(x, 2)
    owns, guest = owner == 1, owner == 0
    mine = x // 2 * 4 + rest
    host = x // 2 * 4 + rest

    def owner_at(index):
        return (index // 4 * 2 + 1) * 4 + lax.rem(index, 4)

    def cube(bit):
        if bit == 3:
            return {"blk": owner_at(mine + 4 * (3 - 2 * (mine // 4)))}
        size = 2**bit
        return {"blk": owner_at(mine + size * (1 - 2 * lax.rem(mine // size, 2)))}

    def guest_at():
        return {"blk": me - 4}

    def signal(sem, peer):
        pl.semaphore_signal(sem, inc=1, device_id=peer, device_id_type=mesh_id)

    loads = [
        pltpu.make_async_copy(src, dst, load_sem.at[i])
        for i, (src, dst) in enumerate(
            ((vel_in, vel), (sc_in, sc), (tab_in, tab), (base_in, base), (frac_in, frac))
        )
    ]
    loads[0].start()

    barrier = pltpu.get_barrier_semaphore()
    near = (
        {"dep": lax.rem(dep + 1, n_dep)},
        {"dep": lax.rem(dep + n_dep - 1, n_dep)},
        {"grp": lax.rem(grp + 1, n_grp)},
        {"grp": lax.rem(grp + n_grp - 1, n_grp)},
        {"blk": lax.rem(me + 1, GROUP)},
        {"blk": lax.rem(me + GROUP - 1, GROUP)},
    )
    up, down = dep // (n_dep - 1), (dep + n_dep - 1) // n_dep
    high, middle = grp // 2, lax.rem((grp + 1) // 2, 2)
    turned = (dep + n_dep - 1) // n_dep
    ahead = 1 - lax.rem(me, 2) + turned * (me // (GROUP - 1))
    behind = 1 - lax.rem(me, 2) - turned * ((GROUP - me) // GROUP)
    first = (up, down, high, middle, ahead, behind)
    for i in range(6):

        @pl.when(first[i] == 0)
        def _():
            signal(barrier, near[i])

    def greet(j, carry):
        signal(barrier, {"blk": j + (j - me + GROUP) // GROUP})
        return carry

    lax.fori_loop(0, owner * (1 - up) * (GROUP - 1), greet, 0)

    @pl.when(owner * up == 1)
    def _():
        signal(barrier, guest_at())
        for bit in range(4):
            signal(barrier, cube(bit))

    expected = (1 - up) * (16 - owner) + up * (1 + 3 * owner)
    pl.semaphore_wait(barrier, expected + up + down + high + middle + ahead + behind)

    pieces = (
        (sc_in.at[pl.ds(4, 4)], zhalo.at[0]),
        (sc_in.at[pl.ds(0, 4)], zhalo.at[1]),
        (ysend.at[0], yhalo.at[0]),
        (ysend.at[1], yhalo.at[1]),
        (xsend.at[0], xhalo.at[0]),
        (xsend.at[1], xhalo.at[1]),
    )
    halos = [
        pltpu.make_async_remote_copy(
            src_ref=src, dst_ref=dst, send_sem=h_send.at[i], recv_sem=h_recv.at[i],
            device_id=near[i], device_id_type=mesh_id,
        )
        for i, (src, dst) in enumerate(pieces)
    ]

    def send_first(indices):
        for i in indices:

            @pl.when(first[i] == 1)
            def _():
                halos[i].start()

    def reply(indices):
        for i in indices:

            @pl.when(first[i] == 0)
            def _():
                halos[i ^ 1].wait_recv()
                halos[i].start()

    def receive(indices):
        for i in indices:

            @pl.when(first[i] == 1)
            def _():
                halos[i ^ 1].wait_recv()

    def piece(buffer, index):
        start = index * 16 if isinstance(index, int) else pl.multiple_of(index * 16, 16)
        return buffer.at[pl.ds(start, 16)]

    def to_owner(start):
        def step(j, carry):
            index = lax.rem(start + j, 16)
            pltpu.make_async_remote_copy(
                src_ref=piece(send1, index), dst_ref=piece(recv1, me), send_sem=a_send, recv_sem=a_recv,
                device_id={"blk": owner_at(index)}, device_id_type=mesh_id,
            ).start()
            return carry

        return step

    def to_column(column):
        for r in range(4):
            peer = 4 * column + r

            @pl.when(me != peer)
            def _():
                pltpu.make_async_remote_copy(
                    src_ref=piece(send2, peer), dst_ref=piece(recv2, mine), send_sem=b_send, recv_sem=b_recv,
                    device_id={"blk": peer}, device_id_type=mesh_id,
                ).start()

    def settle(buffer, count, sem):
        part = buffer.at[pl.ds(0, 16 * count)]
        pltpu.make_async_copy(part, part, sem).wait()

    @pl.when((1 - owner) * up == 1)
    def _():
        signal(hello, {"blk": owner_at(host)})

    @pl.when(owner * up == 1)
    def _():
        signal(met.at[0], cube(0))

    send_first((0, 1))
    loads[0].wait()
    for i in (1, 3, 4):
        loads[i].start()
    pack_velocity(vel, send1)

    @pl.when((1 - owner) * up == 1)
    def _():
        pl.semaphore_wait(go, 1)

    @pl.when(owner * up == 1)
    def _():
        for bit in range(4):
            pl.semaphore_wait(met.at[bit], 1)
            if bit < 3:
                signal(met.at[bit + 1], cube(bit + 1))

    lax.fori_loop(0, 16 - owner, to_owner(owner * (mine + 1) + 4 * (1 - owner)), 0)

    @pl.when(owner * up == 1)
    def _():
        pl.semaphore_wait(hello, 1)
        signal(go, guest_at())

    @pl.when(owns)
    def _():
        loads[2].start()

    loads[1].wait()
    for h in range(2):
        ysend[0, :, 4 * h : 4 * h + 4, :] = sc[4 * h : 4 * h + 4, 28:32, :]
        ysend[1, :, 4 * h : 4 * h + 4, :] = sc[4 * h : 4 * h + 4, 0:4, :]
    flat = sc[...].reshape(TILE, TILE)
    xsend[0] = flat[:, 128:].T[120:]
    xsend[1] = flat[:, :128].T[:8]
    send_first((4, 5, 2, 3))
    reply((4, 5))

    @pl.when(owns)
    def _():
        loads[2].wait()
        recv1[pl.ds(pl.multiple_of(me * 16, 16), 16), :] = send1[pl.ds(pl.multiple_of(mine * 16, 16), 16), :]
        settle(recv1, GROUP - 1, a_recv)
        spectral_segment(recv1, tab, rows, raw, prod, send2, to_column)
        recv2[pl.ds(pl.multiple_of(mine * 16, 16), 16), :] = send2[pl.ds(pl.multiple_of(me * 16, 16), 16), :]

    reply((2, 3, 0))
    loads[3].wait()
    loads[4].wait()
    spline = spline_matrix(base[...], frac[...], me * GROUP)
    for c in range(3):
        weights_out[c] = spline[c]
    receive((4, 5, 2, 3))
    ypad[:, 8:40, :] = sc[...]
    for h in range(2):
        at = slice(4 * h, 4 * h + 4)
        ypad[at, 4:8, :] = yhalo[0, :, at, :]
        ypad[at, 40:44, :] = yhalo[1, :, at, :]
    stencils_xy(sc, ypad, xhalo, slopes, still)
    reply((1,))
    receive((0, 1))
    stencils_z(sc, zhalo, slopes, still)

    @pl.when(owns)
    def _():
        settle(recv2, 15, b_recv)
        settle(send1, 15, a_send)
        settle(send2, GROUP - 1, b_send)

    @pl.when(guest)
    def _():
        settle(recv2, 16, b_recv)
        settle(send1, 16, a_send)

    tiles_out[...] = recv2[...]
    for copy in halos:
        copy.wait_send()


def per_device(velocity, scalar, spline_base, spline_frac):
    vmem = pl.BlockSpec(memory_space=pltpu.VMEM)
    hbm = pl.BlockSpec(memory_space=pltpu.HBM)
    tables = jnp.asarray(spectral_tables())
    parts = pl.pallas_call(
        kernel,
        out_shape=(
            jax.ShapeDtypeStruct((TILE, 128), f32),
            jax.ShapeDtypeStruct((3, 128, TILE), f32),
            jax.ShapeDtypeStruct((3, 8, 32, TILE), f32),
            jax.ShapeDtypeStruct((8, 32, TILE), f32),
        ),
        in_specs=[hbm] * 5,
        out_specs=(vmem,) * 4,
        scratch_shapes=[
            pltpu.VMEM((768, 32), f32),
            pltpu.VMEM((8, 32, TILE), f32),
            pltpu.VMEM((TILE, 4 * LENGTH), bf16),
            pltpu.VMEM((1, TILE), jnp.int32),
            pltpu.VMEM((1, TILE), f32),
            pltpu.VMEM((TILE, 128), f32),
            pltpu.VMEM((2 * TILE, 128), f32),
            pltpu.VMEM((2 * TILE, 128), f32),
            pltpu.VMEM((TILE, 128), f32),
            pltpu.VMEM((192, TILE), f32),
            pltpu.VMEM((3, 16, LENGTH), f32),
            pltpu.VMEM((192, 2 * LENGTH), f32),
            pltpu.VMEM((2, 4, 32, TILE), f32),
            pltpu.VMEM((2, 4, 8, TILE), f32),
            pltpu.VMEM((2, 4, 8, TILE), f32),
            pltpu.VMEM((8, 48, TILE), f32),
            pltpu.VMEM((2, 8, TILE), f32),
            pltpu.VMEM((2, 8, TILE), f32),
            pltpu.SemaphoreType.DMA((5,)),
            pltpu.SemaphoreType.DMA,
            pltpu.SemaphoreType.DMA,
            pltpu.SemaphoreType.DMA,
            pltpu.SemaphoreType.DMA,
            pltpu.SemaphoreType.DMA((6,)),
            pltpu.SemaphoreType.DMA((6,)),
            pltpu.SemaphoreType.REGULAR,
            pltpu.SemaphoreType.REGULAR,
            pltpu.SemaphoreType.REGULAR((4,)),
        ],
        compiler_params=pltpu.CompilerParams(
            collective_id=0, has_side_effects=True, vmem_limit_bytes=24 * 2**20
        ),
        name="segment",
    )(
        *(
            pltpu.with_memory_space_constraint(x, pltpu.HBM)
            for x in (
                velocity.reshape(768, 32),
                scalar,
                spline_base.reshape(1, TILE),
                spline_frac.reshape(1, TILE),
                tables,
            )
        )
    )
    segment, out = pl.pallas_call(
        tail,
        out_shape=(
            jax.ShapeDtypeStruct((768, 32), f32),
            jax.ShapeDtypeStruct((8, 32, TILE), f32),
        ),
        in_specs=[vmem] * 4,
        out_specs=(hbm, hbm),
        scratch_shapes=[
            pltpu.VMEM((TILE, 128), f32),
            pltpu.VMEM((768, 32), f32),
            pltpu.VMEM((8, 32, TILE), f32),
            pltpu.SemaphoreType.DMA((3,)),
        ],
        compiler_params=pltpu.CompilerParams(vmem_limit_bytes=24 * 2**20),
        name="tail",
    )(*parts)
    return segment.reshape(velocity.shape), out


def solution(mesh):
    in_specs = (P(None, "blk", "dep", "grp"), P("dep", "grp", "blk"), P("blk"), P("blk"))
    out_specs = (P(None, "blk", "dep", "grp"), P("dep", "grp", "blk"))
    return jax.shard_map(
        per_device, mesh=mesh, in_specs=in_specs, out_specs=out_specs, check_vma=False
    )
```

```python
import math

import jax
import jax.numpy as jnp
import numpy as np
from jax import lax
from jax.experimental import pallas as pl
from jax.experimental.pallas import tpu as pltpu
from jax.sharding import PartitionSpec as P

velocity_step = 0.002
viscosity = 0.00125
advect_rate = 0.2
diffuse_rate = 0.05
first_coeffs = (0.8, -0.2, 4.0 / 105.0, -1.0 / 280.0)
second_coeffs = (1.6, -0.2, 8.0 / 315.0, -1.0 / 560.0)
second_centre = -205.0 / 72.0

LENGTH = 1024
GROUP = 32
TILE = 256
f32, bf16 = jnp.float32, jnp.bfloat16


def spectral_tables():
    offset = (np.arange(LENGTH)[None, :] - np.arange(TILE)[:, None]) % LENGTH
    angle = np.pi * offset / LENGTH
    parity = 1.0 - 2.0 * (offset % 2)
    same = offset == 0
    sine = np.where(same, 1.0, np.sin(angle))
    first = np.where(same, 0.0, 0.5 * parity * np.cos(angle) / sine)
    second = np.where(same, -(LENGTH**2) / 12.0 - 1.0 / 6.0, -0.5 * parity / sine**2)
    table = np.concatenate([velocity_step * first, velocity_step * viscosity * second], axis=1)
    high = table.astype(np.float32).astype(jnp.bfloat16)
    low = (table - high.astype(np.float64)).astype(np.float32).astype(jnp.bfloat16)
    return np.concatenate([high, low], axis=1)


def split(value):
    high = value.astype(bf16)
    return high, (value - high.astype(f32)).astype(bf16)


def swap_groups(tiles, lane):
    out = []
    for r in range(4):
        value = tiles[r]
        for c in range(4):
            if c == r:
                continue
            moved = pltpu.roll(tiles[c], (32 * (c - r)) % 128, axis=1)
            value = jnp.where(lane // 32 == c, moved, value)
        out.append(value)
    return out


def shift_lanes(tiles, amount):
    lane = lax.broadcasted_iota(jnp.int32, (8, 128), 1)
    count = len(tiles)
    rolled = [pltpu.roll(tile, amount % 128, axis=1) for tile in tiles]
    if amount > 0:
        return [jnp.where(lane < amount, rolled[i - 1], rolled[i]) for i in range(count)]
    edge = 128 + amount
    return [jnp.where(lane < edge, rolled[i], rolled[(i + 1) % count]) for i in range(count)]


def pack_velocity(vel, send):
    for z in range(8):
        part = vel[pl.ds(z, 96, stride=8), :]
        part = jnp.concatenate([part, jnp.zeros((32, 32), f32)], axis=0)
        send[pl.ds(z, 32, stride=8), :] = part.T


def spectral_segment(recv, table, rows, raw, prod, send, dispatch):
    lane = lax.broadcasted_iota(jnp.int32, (8, 128), 1)
    totals = [[None] * 3, [None] * 3]
    for y in range(2):
        own = slice(8 * y, 8 * y + 8)
        for x in range(8):
            tiles = [recv[(4 * x + r) * 16 + 8 * y : (4 * x + r) * 16 + 8 * y + 8, :] for r in range(4)]
            got = swap_groups(tiles, lane)
            for c in range(3):
                raw[c, own, 128 * x : 128 * x + 128] = got[c]
                totals[y][c] = got[c] if x == 0 else totals[y][c] + got[c]
    for y in range(2):
        own = slice(8 * y, 8 * y + 8)
        for c in range(3):
            mean = jnp.sum(totals[y][c], axis=1, keepdims=True) * (1.0 / LENGTH)
            for j in range(4):
                at = j * 48 + c * 16 + 8 * y
                rows[at : at + 8, :] = raw[c, own, TILE * j : TILE * j + TILE] - mean
    high, low = split(rows[...])
    both = jnp.concatenate([high, low], axis=0)
    for m in range(8):
        cols = slice(TILE * m, TILE * m + TILE)
        lows = slice(2 * LENGTH + TILE * m, 2 * LENGTH + TILE * m + TILE)
        main = jnp.dot(both, table[:, cols], preferred_element_type=f32)
        rest = jnp.dot(high, table[:, lows], preferred_element_type=f32)
        prod[:, cols] = main[:192] + main[192:] + rest
    within = lane % 32
    packed = []
    for y in range(2):
        segment = [[], [], []]
        for k in range(4):
            speed = raw[0, 8 * y : 8 * y + 8, TILE * k : TILE * k + TILE]
            for c in range(3):
                first = second = None
                for j in range(4):
                    m = (k - j) % 4
                    at = slice(j * 48 + c * 16 + 8 * y, j * 48 + c * 16 + 8 * y + 8)
                    a = prod[at, TILE * m : TILE * m + TILE]
                    b = prod[at, LENGTH + TILE * m : LENGTH + TILE * m + TILE]
                    first = a if j == 0 else first + a
                    second = b if j == 0 else second + b
                at = k * 48 + c * 16 + 8 * y
                value = rows[at : at + 8, :] + (second - speed * first)
                segment[c] += [value[:, :128], value[:, 128:]]
        halo = [jnp.zeros((8, 128), f32)] * 8
        for c in range(3):
            low_side = shift_lanes(segment[c], 2 + 4 * c)
            high_side = shift_lanes(segment[c], -30 + 4 * c)
            for x in range(8):
                halo[x] = jnp.where(within // 2 == 2 * c, low_side[x], halo[x])
                halo[x] = jnp.where(within // 2 == 2 * c + 1, high_side[x], halo[x])
        packed.append(segment + [halo])
    order = (0, 1, 7, 2, 6, 3, 5, 4)
    for i, x in enumerate(order):
        for y in range(2):
            tiles = swap_groups([packed[y][c][x] for c in range(4)], lane)
            for r in range(4):
                at = (4 * x + r) * 16 + 8 * y
                send[at : at + 8, :] = tiles[r]
        if i > 0:
            dispatch(order[i - 1])
    dispatch(order[-1])


def spline_matrix(base, frac, first_cell):
    row = lax.broadcasted_iota(jnp.int32, (128, TILE), 0)
    side = row - 96
    halo = side % 4
    slot = jnp.where(row < 96, row % 32 + 2, jnp.where(halo < 2, halo, halo + 32))
    owner = jnp.where(row < 96, row // 32, side // 4)
    local = base - (first_cell - 2)
    square = frac * frac
    cube = square * frac
    weights = (
        (-cube + 2.0 * square - frac) * 0.5,
        (3.0 * cube - 5.0 * square + 2.0) * 0.5,
        (-3.0 * cube + 4.0 * square + frac) * 0.5,
        (cube - square) * 0.5,
    )
    matrix = jnp.zeros((128, TILE), f32)
    for tap in range(4):
        matrix = matrix + jnp.where(slot == local + (tap - 1), weights[tap], 0.0)
    return [jnp.where(owner == c, matrix, 0.0) for c in range(3)]


def pair_sums(window):
    slope = curve = None
    for m in range(1, 5):
        ahead, behind = window(m), window(-m)
        a = first_coeffs[m - 1] * (ahead - behind)
        b = second_coeffs[m - 1] * (ahead + behind)
        slope = a if m == 1 else slope + a
        curve = b if m == 1 else curve + b
    return slope, curve


def stencils_xy(sc, ypad, xhalo, slopes, still):
    pad = jnp.zeros((120, TILE), f32)
    left = jnp.concatenate([pad, xhalo[0]], axis=0).T
    right = jnp.concatenate([xhalo[1], pad], axis=0).T
    for z in range(8):
        own = sc[z]

        def along_y(m):
            return ypad[z, 8 + m : 40 + m, :]

        wide = jnp.concatenate([left[32 * z : 32 * z + 32], own, right[32 * z : 32 * z + 32]], axis=1)

        def along_x(m):
            return pltpu.roll(wide, (-m) % 512, axis=1)[:, 128:384]

        slope_y, curve_y = pair_sums(along_y)
        slope_x, curve_x = pair_sums(along_x)
        curve = curve_y + curve_x + (3.0 * second_centre) * own
        still[z] = own + diffuse_rate * curve
        slopes[0, z] = advect_rate * slope_x
        slopes[1, z] = advect_rate * slope_y


def stencils_z(sc, zhalo, slopes, still):
    for z in range(8):

        def along_z(m):
            at = z + m
            if at < 0:
                return zhalo[0, 4 + at]
            return zhalo[1, at - 8] if at >= 8 else sc[at]

        slope_z, curve_z = pair_sums(along_z)
        still[z] = still[z] + diffuse_rate * curve_z
        slopes[2, z] = advect_rate * slope_z


def tail(tiles, weights, slopes, still, seg_out, sc_out, lhs, seg, sc, sems):
    for z in range(8):
        tile = tiles[pl.ds(z, 32, stride=8), :]
        lhs[32 * z : 32 * z + 32, :] = tile
        seg[pl.ds(z, 96, stride=8), :] = tile.T[:96]
    high, low = split(lhs[...])
    both = jnp.concatenate([high, low], axis=1)
    copies = [pltpu.make_async_copy(seg, seg_out, sems.at[0])]
    copies[0].start()
    fine = []
    for c in range(3):
        w_high, w_low = split(weights[c])
        fine.append(
            jnp.dot(both, jnp.concatenate([w_high, w_high], axis=0), preferred_element_type=f32)
            + jnp.dot(high, w_low, preferred_element_type=f32)
        )
    for z in range(8):
        at = slice(32 * z, 32 * z + 32)
        moved = fine[0][at] * slopes[0, z] + fine[1][at] * slopes[1, z] + fine[2][at] * slopes[2, z]
        sc[z] = still[z] - moved
        if z % 4 == 3:
            half = pl.ds(z - 3, 4)
            copies.append(pltpu.make_async_copy(sc.at[half], sc_out.at[half], sems.at[1 + z // 4]))
            copies[-1].start()
    for copy in copies:
        copy.wait()


def kernel(
    vel_in, sc_in, base_in, frac_in, tab_in, tiles_out, weights_out, slopes, still,
    vel, sc, tab, base, frac, send1, recv1, send2, recv2, rows, raw, prod,
    zhalo, ysend, yhalo, ypad, xsend, xhalo,
    load_sem, a_send, a_recv, b_send, b_recv, h_send, h_recv, hello, go, met,
):
    me = lax.axis_index("blk")
    grp, dep = lax.axis_index("grp"), lax.axis_index("dep")
    n_grp, n_dep = lax.axis_size("grp"), lax.axis_size("dep")
    mesh_id = pl.DeviceIdType.MESH
    x, rest = me // 4, lax.rem(me, 4)
    owner = lax.rem(x, 2)
    owns, guest = owner == 1, owner == 0
    mine = x // 2 * 4 + rest
    host = x // 2 * 4 + rest

    def owner_at(index):
        return (index // 4 * 2 + 1) * 4 + index % 4

    def cube(bit):
        if bit == 3:
            return {"blk": owner_at(mine + 4 * (3 - 2 * (mine // 4)))}
        size = 2**bit
        return {"blk": owner_at(mine + size * (1 - 2 * lax.rem(mine // size, 2)))}

    def guest_at():
        return {"blk": me - 4}

    def signal(sem, peer):
        pl.semaphore_signal(sem, inc=1, device_id=peer, device_id_type=mesh_id)

    loads = [
        pltpu.make_async_copy(src, dst, load_sem.at[i])
        for i, (src, dst) in enumerate(
            ((vel_in, vel), (sc_in, sc), (tab_in, tab), (base_in, base), (frac_in, frac))
        )
    ]
    loads[0].start()

    barrier = pltpu.get_barrier_semaphore()
    near = (
        {"dep": lax.rem(dep + 1, n_dep)},
        {"dep": lax.rem(dep + n_dep - 1, n_dep)},
        {"grp": lax.rem(grp + 1, n_grp)},
        {"grp": lax.rem(grp + n_grp - 1, n_grp)},
        {"blk": lax.rem(me + 1, GROUP)},
        {"blk": lax.rem(me + GROUP - 1, GROUP)},
    )
    up, down = dep // (n_dep - 1), (dep + n_dep - 1) // n_dep
    high, middle = grp // 2, lax.rem((grp + 1) // 2, 2)
    turned = (dep + n_dep - 1) // n_dep
    ahead = 1 - lax.rem(me, 2) + turned * (me // (GROUP - 1))
    behind = 1 - lax.rem(me, 2) - turned * ((GROUP - me) // GROUP)
    first = (up, down, high, middle, ahead, behind)
    for i in range(6):

        @pl.when(first[i] == 0)
        def _():
            signal(barrier, near[i])

    def greet(j, carry):
        signal(barrier, {"blk": j + (j - me + GROUP) // GROUP})
        return carry

    lax.fori_loop(0, owner * (1 - up) * (GROUP - 1), greet, 0)

    @pl.when(owner * up == 1)
    def _():
        signal(barrier, guest_at())
        for bit in range(4):
            signal(barrier, cube(bit))

    expected = (1 - up) * (16 - owner) + up * (1 + 3 * owner)
    pl.semaphore_wait(barrier, expected + up + down + high + middle + ahead + behind)

    pieces = (
        (sc_in.at[pl.ds(4, 4)], zhalo.at[0]),
        (sc_in.at[pl.ds(0, 4)], zhalo.at[1]),
        (ysend.at[0], yhalo.at[0]),
        (ysend.at[1], yhalo.at[1]),
        (xsend.at[0], xhalo.at[0]),
        (xsend.at[1], xhalo.at[1]),
    )
    halos = [
        pltpu.make_async_remote_copy(
            src_ref=src, dst_ref=dst, send_sem=h_send.at[i], recv_sem=h_recv.at[i],
            device_id=near[i], device_id_type=mesh_id,
        )
        for i, (src, dst) in enumerate(pieces)
    ]

    def send_first(indices):
        for i in indices:

            @pl.when(first[i] == 1)
            def _():
                halos[i].start()

    def reply(indices):
        for i in indices:

            @pl.when(first[i] == 0)
            def _():
                halos[i ^ 1].wait_recv()
                halos[i].start()

    def receive(indices):
        for i in indices:

            @pl.when(first[i] == 1)
            def _():
                halos[i ^ 1].wait_recv()

    def piece(buffer, index):
        start = index * 16 if isinstance(index, int) else pl.multiple_of(index * 16, 16)
        return buffer.at[pl.ds(start, 16)]

    def give(index):
        pltpu.make_async_remote_copy(
            src_ref=piece(send1, index), dst_ref=piece(recv1, me), send_sem=a_send, recv_sem=a_recv,
            device_id={"blk": owner_at(index)}, device_id_type=mesh_id,
        ).start()

    def to_owner(j, carry):
        give(lax.rem(mine + 1 + j, 16))
        return carry

    def to_column(column):
        for r in range(4):
            peer = 4 * column + r

            @pl.when(me != peer)
            def _():
                pltpu.make_async_remote_copy(
                    src_ref=piece(send2, peer), dst_ref=piece(recv2, mine), send_sem=b_send, recv_sem=b_recv,
                    device_id={"blk": peer}, device_id_type=mesh_id,
                ).start()

    def settle(buffer, count, sem):
        part = buffer.at[pl.ds(0, 16 * count)]
        pltpu.make_async_copy(part, part, sem).wait()

    @pl.when((1 - owner) * up == 1)
    def _():
        signal(hello, {"blk": owner_at(host)})

    @pl.when(owner * up == 1)
    def _():
        signal(met.at[0], cube(0))

    send_first((0, 1))
    loads[0].wait()
    for i in (1, 3, 4):
        loads[i].start()
    pack_velocity(vel, send1)

    @pl.when((1 - owner) * up == 1)
    def _():
        pl.semaphore_wait(go, 1)

    @pl.when(owner * up == 1)
    def _():
        for bit in range(4):
            pl.semaphore_wait(met.at[bit], 1)
            if bit < 3:
                signal(met.at[bit + 1], cube(bit + 1))

    @pl.when(guest)
    def _():
        for index in (4, 5, 6, 7, 8, 9, 10, 11, 12, 13, 14, 15, 0, 1, 2, 3):
            give(index)

    @pl.when(owns)
    def _():
        lax.fori_loop(0, 15, to_owner, 0)


    @pl.when(owner * up == 1)
    def _():
        pl.semaphore_wait(hello, 1)
        signal(go, guest_at())

    @pl.when(owns)
    def _():
        loads[2].start()

    loads[1].wait()
    for h in range(2):
        ysend[0, :, 4 * h : 4 * h + 4, :] = sc[4 * h : 4 * h + 4, 28:32, :]
        ysend[1, :, 4 * h : 4 * h + 4, :] = sc[4 * h : 4 * h + 4, 0:4, :]
    flat = sc[...].reshape(TILE, TILE)
    xsend[0] = flat[:, 128:].T[120:]
    xsend[1] = flat[:, :128].T[:8]
    send_first((4, 5, 2, 3))
    reply((4, 5))

    @pl.when(owns)
    def _():
        loads[2].wait()
        recv1[pl.ds(pl.multiple_of(me * 16, 16), 16), :] = send1[pl.ds(pl.multiple_of(mine * 16, 16), 16), :]
        settle(recv1, GROUP - 1, a_recv)
        spectral_segment(recv1, tab, rows, raw, prod, send2, to_column)
        recv2[pl.ds(pl.multiple_of(mine * 16, 16), 16), :] = send2[pl.ds(pl.multiple_of(me * 16, 16), 16), :]

    reply((2, 3, 0))
    loads[3].wait()
    loads[4].wait()
    spline = spline_matrix(base[...], frac[...], me * GROUP)
    for c in range(3):
        weights_out[c] = spline[c]
    receive((4, 5, 2, 3))
    ypad[:, 8:40, :] = sc[...]
    for h in range(2):
        at = slice(4 * h, 4 * h + 4)
        ypad[at, 4:8, :] = yhalo[0, :, at, :]
        ypad[at, 40:44, :] = yhalo[1, :, at, :]
    stencils_xy(sc, ypad, xhalo, slopes, still)
    reply((1,))
    receive((0, 1))
    stencils_z(sc, zhalo, slopes, still)

    @pl.when(owns)
    def _():
        settle(recv2, 15, b_recv)
        settle(send1, 15, a_send)
        settle(send2, GROUP - 1, b_send)

    @pl.when(guest)
    def _():
        settle(recv2, 16, b_recv)
        settle(send1, 16, a_send)

    tiles_out[...] = recv2[...]
    for copy in halos:
        copy.wait_send()


def per_device(velocity, scalar, spline_base, spline_frac):
    vmem = pl.BlockSpec(memory_space=pltpu.VMEM)
    hbm = pl.BlockSpec(memory_space=pltpu.HBM)
    tables = jnp.asarray(spectral_tables())
    parts = pl.pallas_call(
        kernel,
        out_shape=(
            jax.ShapeDtypeStruct((TILE, 128), f32),
            jax.ShapeDtypeStruct((3, 128, TILE), f32),
            jax.ShapeDtypeStruct((3, 8, 32, TILE), f32),
            jax.ShapeDtypeStruct((8, 32, TILE), f32),
        ),
        in_specs=[hbm] * 5,
        out_specs=(vmem,) * 4,
        scratch_shapes=[
            pltpu.VMEM((768, 32), f32),
            pltpu.VMEM((8, 32, TILE), f32),
            pltpu.VMEM((TILE, 4 * LENGTH), bf16),
            pltpu.VMEM((1, TILE), jnp.int32),
            pltpu.VMEM((1, TILE), f32),
            pltpu.VMEM((TILE, 128), f32),
            pltpu.VMEM((2 * TILE, 128), f32),
            pltpu.VMEM((2 * TILE, 128), f32),
            pltpu.VMEM((TILE, 128), f32),
            pltpu.VMEM((192, TILE), f32),
            pltpu.VMEM((3, 16, LENGTH), f32),
            pltpu.VMEM((192, 2 * LENGTH), f32),
            pltpu.VMEM((2, 4, 32, TILE), f32),
            pltpu.VMEM((2, 4, 8, TILE), f32),
            pltpu.VMEM((2, 4, 8, TILE), f32),
            pltpu.VMEM((8, 48, TILE), f32),
            pltpu.VMEM((2, 8, TILE), f32),
            pltpu.VMEM((2, 8, TILE), f32),
            pltpu.SemaphoreType.DMA((5,)),
            pltpu.SemaphoreType.DMA,
            pltpu.SemaphoreType.DMA,
            pltpu.SemaphoreType.DMA,
            pltpu.SemaphoreType.DMA,
            pltpu.SemaphoreType.DMA((6,)),
            pltpu.SemaphoreType.DMA((6,)),
            pltpu.SemaphoreType.REGULAR,
            pltpu.SemaphoreType.REGULAR,
            pltpu.SemaphoreType.REGULAR((4,)),
        ],
        compiler_params=pltpu.CompilerParams(
            collective_id=0, has_side_effects=True, vmem_limit_bytes=24 * 2**20
        ),
        name="segment",
    )(
        *(
            pltpu.with_memory_space_constraint(x, pltpu.HBM)
            for x in (
                velocity.reshape(768, 32),
                scalar,
                spline_base.reshape(1, TILE),
                spline_frac.reshape(1, TILE),
                tables,
            )
        )
    )
    segment, out = pl.pallas_call(
        tail,
        out_shape=(
            jax.ShapeDtypeStruct((768, 32), f32),
            jax.ShapeDtypeStruct((8, 32, TILE), f32),
        ),
        in_specs=[vmem] * 4,
        out_specs=(hbm, hbm),
        scratch_shapes=[
            pltpu.VMEM((TILE, 128), f32),
            pltpu.VMEM((768, 32), f32),
            pltpu.VMEM((8, 32, TILE), f32),
            pltpu.SemaphoreType.DMA((3,)),
        ],
        compiler_params=pltpu.CompilerParams(vmem_limit_bytes=24 * 2**20),
        name="tail",
    )(*parts)
    return segment.reshape(velocity.shape), out


def solution(mesh):
    in_specs = (P(None, "blk", "dep", "grp"), P("dep", "grp", "blk"), P("blk"), P("blk"))
    out_specs = (P(None, "blk", "dep", "grp"), P("dep", "grp", "blk"))
    return jax.shard_map(
        per_device, mesh=mesh, in_specs=in_specs, out_specs=out_specs, check_vma=False
    )
```
